32 devices in a mesh: gx: 8 (over z, y), gy: 4 (over x, core).
Axes of the slice: x: 2, y: 2, z: 4, core: 2. Of those that a mesh axis runs over, the one named last changes fastest.
Arguments:
- source_term: float32 [256, 128, 256], P('gx', 'gy'), may hold values from -6 to 6
- mobility_x: float32 [256, 128, 256], P('gx', 'gy'), may hold values from 0.001 to 1
- mobility_y: float32 [256, 128, 256], P('gx', 'gy'), may hold values from 0.001 to 1
- mobility_z: float32 [256, 128, 256], P('gx', 'gy'), may hold values from 0.001 to 1
- bubble_fraction: float32 [256, 128, 256], P('gx', 'gy'), may hold values from 0.1 to 1
- tile_labels: int32 [256, 128, 2], P('gx', 'gy'), may hold values from 0 to 65535, as said below
- send_tiles: int32 [32, 32, 128], P(('gx', 'gy')), may hold values from 0 to 2048, as said below
- recv_rows: int32 [32, 32, 128], P(('gx', 'gy')), may hold values from 0 to 2048, as said below
- block_inverse: float32 [512, 128, 128], P(('gx', 'gy'))
- couplings: float32 [512, 2, 128, 128], P(('gx', 'gy')), may hold values from -0.05303301 to 0.05303301
- neighbours: int32 [512, 2], P(('gx', 'gy')), may hold values from 0 to 511, as said below
Outputs:
- solution_field: float32 [256, 128, 256], P('gx', 'gy')
- residual: float32 [256, 128, 256], P('gx', 'gy')
The draws below stay inside these ranges and needn't reach their ends.
Inputs may be any that keep to these rules, and one draw needn't show every extreme that they name: The tile_labels entry of a tile is o * 2048 + r exactly where its device s lists it in send_tiles[s, o, n] and recv_rows[o, s, n] = r; every tile is listed once. send_tiles[s, o, n] is a tile number of device s, or 2048 for an empty slot; the filled slots of each s and o come first; one owner receives 128 filled slots from every device. recv_rows[o, s, n] is the owned row that slot n from device s adds into, or 2048 where that slot is empty. Block q belongs to device q // 16. neighbours[q, n] is a block of another device. The entries listed by the blocks of one device name blocks of exactly 8 distinct devices, exactly 4 entries for each of them.
All inputs are finite; a program needn't handle non-finite values.
Results may differ from the reference program's by a relative error of at most 0.00012.
Values sent between devices are 32-bit elements; how exact they have to be, the bound alone decides.
A program may use at most 64 MiB of HBM per device.

```python
import math
import jax
import jax.numpy as jnp
from jax import lax

CX = 32
CY = 32
NZ = 256
TZ = 128
NB_DEV = 2048
CB = 128
NBR = 2
LINK = 4
ITERS = 2
NX = 256
NY = 128
NZT = 2
TPD = 2048
NB = 65536
BPD = 16
NBLK = 512
MEAN = 64
CAP = 128
N_GX = 8
N_GY = 4
DEVICES = 32


def owner_layout(key):
    base_key = jax.random.fold_in(key, 11)
    key_pairing, key_surplus, key_shuffle, key_rows = jax.random.split(base_key, 4)
    half_count = DEVICES // 2
    pairing = jax.random.permutation(key_pairing, DEVICES).astype(jnp.int32)
    front_owner = pairing[half_count]
    second = pairing[half_count + 1]
    swapped = front_owner == DEVICES - 1
    pairing = pairing.at[half_count].set(jnp.where(swapped, second, front_owner))
    pairing = pairing.at[half_count + 1].set(jnp.where(swapped, front_owner, second))
    surplus = jax.random.randint(key_surplus, (DEVICES, half_count), 0, MEAN + 1)
    surplus = surplus.at[:, 0].set(MEAN)
    ranked = jnp.concatenate([MEAN + surplus, MEAN - surplus], axis=1).astype(jnp.int32)
    counts = jnp.zeros((DEVICES, DEVICES), jnp.int32).at[:, pairing].set(ranked)
    run_ends = jnp.cumsum(counts, axis=1)
    starts = run_ends - counts
    places = jnp.arange(TPD, dtype=jnp.int32)
    owners = jax.vmap(lambda run_row: jnp.searchsorted(run_row, places, side='right'))(run_ends).astype(jnp.int32)
    shuffles = jax.vmap(lambda sub_key: jax.random.permutation(sub_key, TPD))(jax.random.split(key_shuffle, DEVICES)).astype(jnp.int32)
    row_ids = jax.random.randint(key_rows, (DEVICES, TPD), 0, NB_DEV)
    run_start = jnp.take_along_axis(starts, owners, axis=1) == places[None, :]
    row_ids = jnp.where(run_start, NB_DEV - 1, row_ids).astype(jnp.int32)
    sources = jnp.arange(DEVICES, dtype=jnp.int32)[:, None]
    tile_label = jnp.zeros((DEVICES, TPD), jnp.int32).at[sources, shuffles].set(owners * NB_DEV + row_ids)
    slot_ids = jnp.arange(CAP, dtype=jnp.int32)
    positions = starts[:, :, None] + slot_ids[None, None, :]
    filled = slot_ids[None, None, :] < counts[:, :, None]
    clipped = jnp.minimum(positions, TPD - 1).reshape(DEVICES, DEVICES * CAP)
    tile_ids = jnp.take_along_axis(shuffles, clipped, axis=1).reshape(DEVICES, DEVICES, CAP)
    picked = jnp.take_along_axis(row_ids, clipped, axis=1).reshape(DEVICES, DEVICES, CAP)
    send_list = jnp.where(filled, tile_ids, TPD).astype(jnp.int32)
    recv_list = jnp.transpose(jnp.where(filled, picked, NB_DEV), (1, 0, 2)).astype(jnp.int32)
    labels = tile_label.reshape(N_GX, N_GY, CX, CY, NZT).transpose(0, 2, 1, 3, 4).reshape(NX, NY, NZT)
    return (labels, send_list, recv_list)


def draw_tile_labels(key, part):
    return owner_layout(key)[0]


def draw_send_tiles(key, part):
    return owner_layout(key)[1]


def draw_recv_rows(key, part):
    return owner_layout(key)[2]


def draw_neighbours(key, part):
    key_offsets, key_order, key_local = jax.random.split(jax.random.fold_in(key, 23), 3)
    push_count = BPD * NBR
    group_count = push_count // LINK
    offset_keys = jax.random.split(key_offsets, DEVICES)
    order_keys = jax.random.split(key_order, DEVICES)
    offsets = jax.vmap(lambda sub_key: jax.random.permutation(sub_key, DEVICES - 1)[:group_count] + 1)(offset_keys).astype(jnp.int32)
    orders = jax.vmap(lambda sub_key: jax.random.permutation(sub_key, push_count))(order_keys).astype(jnp.int32)
    group_of = (orders // LINK).astype(jnp.int32)
    chosen = jnp.take_along_axis(offsets, group_of, axis=1)
    sources = jnp.arange(DEVICES, dtype=jnp.int32)[:, None]
    targets = (sources + chosen) % DEVICES
    local = jax.random.randint(key_local, (DEVICES, push_count), 0, BPD)
    blocks = targets * BPD + local
    return blocks.reshape(NBLK, NBR).astype(jnp.int32)


def draw_block_inverse(key, part):
    key_scale, key_noise = jax.random.split(jax.random.fold_in(key, 31))
    scales = jnp.exp(jax.random.uniform(key_scale, (NBLK, 1, 1), jnp.float32, math.log(0.3), 0.0))
    noise = jax.random.normal(key_noise, (NBLK, CB, CB), jnp.float32)
    mixed = (noise + jnp.swapaxes(noise, 1, 2)) * (0.25 / math.sqrt(2.0 * CB))
    return (scales * (jnp.eye(CB, dtype=jnp.float32)[None] + mixed)).astype(jnp.float32)


def steps_of(stream_key, shape, shards, smallest, largest):
    def one(position, shards_of):
        draws = jax.random.uniform(jax.random.fold_in(jax.random.fold_in(stream_key, 6), position), (shards_of,), jnp.float32, smallest / len(shards), largest / len(shards))
        return jnp.repeat(jnp.exp(draws), shape[position] // shards_of).reshape((-1,) + (1,) * (len(shape) - position - 1))

    loudness = one(*shards[0])
    for cut in shards[1:]:
        loudness = loudness * one(*cut)
    return loudness


def scatter_about(stream_key, shape, width, bound, cuts=(), held_as=jnp.bfloat16):
    loudness = steps_of(stream_key, shape, cuts, -0.22, 0.18) if cuts else 1.0
    array = jax.random.normal(stream_key, shape, jnp.float32) * width * loudness
    return jnp.minimum(jnp.maximum(array, -bound), bound).astype(held_as)


def setup_inputs(seed: int = 0) -> dict:
    seeds = jax.random.split(jax.random.key(seed), 12)
    source_term = scatter_about(seeds[0], (NX, NY, NZ), 1.0, 6.0, ((0, 8), (1, 4)), jnp.float32)
    mobility_x = jnp.clip(jnp.exp(math.log(1.0) - 6.9077552 * jax.random.uniform(seeds[1], (NX, NY, NZ), jnp.float32) ** steps_of(seeds[1], (NX, NY, NZ), ((0, 8), (1, 4)), -0.2, 0.2)), 0.001, 1.0)
    mobility_y = jnp.clip(jnp.exp(math.log(1.0) - 6.9077552 * jax.random.uniform(seeds[2], (NX, NY, NZ), jnp.float32) ** steps_of(seeds[2], (NX, NY, NZ), ((0, 8), (1, 4)), -0.2, 0.2)), 0.001, 1.0)
    mobility_z = jnp.clip(jnp.exp(math.log(1.0) - 6.9077552 * jax.random.uniform(seeds[3], (NX, NY, NZ), jnp.float32) ** steps_of(seeds[3], (NX, NY, NZ), ((0, 8), (1, 4)), -0.2, 0.2)), 0.001, 1.0)
    bubble_fraction = jnp.clip(0.1 + 0.9 * jax.random.uniform(seeds[4], (NX, NY, NZ), jnp.float32) ** steps_of(seeds[4], (NX, NY, NZ), ((0, 8), (1, 4)), -0.2, 0.2), 0.1, 1.0)
    tile_labels = draw_tile_labels(jax.random.fold_in(seeds[11], 71), 0)
    send_tiles = draw_send_tiles(jax.random.fold_in(seeds[11], 71), 0)
    recv_rows = draw_recv_rows(jax.random.fold_in(seeds[11], 71), 0)
    block_inverse = draw_block_inverse(jax.random.fold_in(seeds[11], 71), 0)
    couplings = scatter_about(seeds[9], (NBLK, NBR, CB, CB), (0.1 / CB ** 0.5), 0.05303301, ((0, 32),), jnp.float32)
    neighbours = draw_neighbours(jax.random.fold_in(seeds[11], 71), 0)
    return {"source_term": source_term, "mobility_x": mobility_x, "mobility_y": mobility_y, "mobility_z": mobility_z, "bubble_fraction": bubble_fraction, "tile_labels": tile_labels, "send_tiles": send_tiles, "recv_rows": recv_rows, "block_inverse": block_inverse, "couplings": couplings, "neighbours": neighbours}


def lower_plane(values, axis):
    zero_plane = jnp.zeros_like(lax.slice_in_dim(values, 0, 1, axis=axis))
    return jnp.concatenate([zero_plane, lax.slice_in_dim(values, 0, values.shape[axis] - 1, axis=axis)], axis=axis)


def upper_plane(values, axis):
    zero_plane = jnp.zeros_like(lax.slice_in_dim(values, 0, 1, axis=axis))
    return jnp.concatenate([lax.slice_in_dim(values, 1, values.shape[axis], axis=axis), zero_plane], axis=axis)


def apply_operator(field, mobility_x, mobility_y, mobility_z):
    total_part = None
    for axis, mobility in ((0, mobility_x), (1, mobility_y), (2, mobility_z)):
        flux = mobility * (upper_plane(field, axis) - field)
        part = flux - lower_plane(flux, axis)
        total_part = part if total_part is None else total_part + part
    return -total_part


def restrict(tile_totals, send_tiles, recv_rows):
    per_device = tile_totals.reshape(N_GX, CX, N_GY, CY, NZT).transpose(0, 2, 1, 3, 4).reshape(DEVICES, TPD)
    padded = jnp.concatenate([per_device, jnp.zeros((DEVICES, 1), jnp.float32)], axis=1)
    values = jnp.take_along_axis(padded, send_tiles.reshape(DEVICES, DEVICES * CAP), axis=1)
    row_ids = jnp.transpose(recv_rows, (1, 0, 2))
    owner_ids = jnp.arange(DEVICES, dtype=jnp.int32)[None, :, None]
    target = jnp.where(row_ids < NB_DEV, owner_ids * NB_DEV + row_ids, NB).astype(jnp.int32)
    summed = jax.ops.segment_sum(values.reshape(-1), target.reshape(-1), num_segments=NB + 1)
    return summed[:NB]


def precondition(resid, bubble_fraction, tile_labels, send_tiles, recv_rows, block_inverse, couplings, neighbours, diagonal):
    tile_totals = (bubble_fraction * resid).reshape(NX, NY, NZT, TZ).sum(axis=3)
    totals = restrict(tile_totals, send_tiles, recv_rows).reshape(NBLK, CB)
    sweep_one = jnp.einsum("qij,qj->qi", block_inverse, totals, precision=lax.Precision.HIGHEST)
    pushed = jnp.einsum("qkij,qj->qki", couplings, sweep_one, precision=lax.Precision.HIGHEST)
    coupled = jnp.zeros((NBLK, CB), jnp.float32).at[neighbours.reshape(-1)].add(pushed.reshape(-1, CB))
    sweep_two = jnp.einsum("qij,qj->qi", block_inverse, totals - coupled, precision=lax.Precision.HIGHEST)
    tile_values = sweep_two.reshape(-1)[tile_labels]
    spread = jnp.broadcast_to(tile_values[..., None], (NX, NY, NZT, TZ)).reshape(NX, NY, NZ)
    return bubble_fraction * spread + resid / diagonal


def reference(source_term, mobility_x, mobility_y, mobility_z, bubble_fraction, tile_labels, send_tiles, recv_rows, block_inverse, couplings, neighbours):
    diagonal = (mobility_x + lower_plane(mobility_x, 0)) + (mobility_y + lower_plane(mobility_y, 1)) + (mobility_z + lower_plane(mobility_z, 2))

    def apply_pre(resid):
        return precondition(resid, bubble_fraction, tile_labels, send_tiles, recv_rows, block_inverse, couplings, neighbours, diagonal)

    solution_field = jnp.zeros_like(source_term)
    residual = source_term
    precond = apply_pre(residual)
    direction = precond
    rz_now = jnp.sum(residual * precond)
    for step in range(ITERS):
        image = apply_operator(direction, mobility_x, mobility_y, mobility_z)
        alpha = rz_now / jnp.sum(direction * image)
        solution_field = solution_field + alpha * direction
        residual = residual - alpha * image
        if step + 1 < ITERS:
            precond = apply_pre(residual)
            rz_next = jnp.sum(residual * precond)
            direction = precond + (rz_next / rz_now) * direction
            rz_now = rz_next
    return solution_field, residual
```

```python
import functools

import jax
import jax.numpy as jnp
from jax import lax
from jax.experimental import pallas as pl
from jax.experimental.pallas import tpu as pltpu
from jax.sharding import PartitionSpec as P

TZ = 128
LINK = 4
SLOT = 8
F32 = jnp.float32
BF16 = jnp.bfloat16
HIGHEST = lax.Precision.HIGHEST
MESH = pl.DeviceIdType.MESH
NT = (((1,), (1,)), ((), ()))
NN = (((1,), (0,)), ((), ()))
CELL_ARRAYS = 5


def log2(value):
    assert value & (value - 1) == 0
    return value.bit_length() - 1


def iota(shape, axis):
    return lax.broadcasted_iota(jnp.int32, shape, axis)


def split_three(value, axis=0):
    first = value.astype(BF16)
    rest = value - first.astype(F32)
    second = rest.astype(BF16)
    third = (rest - second.astype(F32)).astype(BF16)
    return jnp.concatenate([first, second, third], axis=axis)


def fold_three(value):
    third = value.shape[0] // 3
    return value[:third] + value[third : 2 * third] + value[2 * third :]


def one_hot_low(index):
    return jnp.where(iota((128, 128), 0) == (index & 127), 1.0, 0.0).astype(BF16)


def gather_rows(table, index_ref, out_ref, unroll):
    parts = split_three(table)
    high_count = table.shape[0]

    def step(block, carry):
        for sub in range(unroll):
            row = block * unroll + sub
            index = index_ref[pl.ds(row, 1), :]
            picked = fold_three(
                lax.dot_general(parts, one_hot_low(index), NN, preferred_element_type=F32)
            )
            hit = iota((high_count, 128), 0) == (index >> 7)
            out_ref[row] = jnp.sum(jnp.where(hit, picked, 0.0), axis=0, keepdims=True)
        return carry

    lax.fori_loop(0, index_ref.shape[0] // unroll, step, 0)


def scatter_rows(value_ref, index_ref, high_count, unroll):
    def step(block, total):
        for sub in range(unroll):
            row = block * unroll + sub
            index = index_ref[pl.ds(row, 1), :]
            hit = iota((high_count, 128), 0) == (index >> 7)
            parts = split_three(jnp.where(hit, value_ref[row], 0.0))
            total = total + lax.dot_general(
                parts, one_hot_low(index), NT, preferred_element_type=F32
            )
        return total

    start = jnp.zeros((3 * high_count, 128), F32)
    return fold_three(lax.fori_loop(0, index_ref.shape[0] // unroll, step, start))


def block_products(vectors, matrix_at, count, per_vector):
    rows = []
    for p in range(count):
        q = p // per_vector
        rows.append(
            lax.dot_general(
                vectors[q : q + 1],
                matrix_at(p),
                NT,
                precision=HIGHEST,
                preferred_element_type=F32,
            )
        )
    return jnp.concatenate(rows, axis=0)


def kernel(
    counts,
    source_hbm,
    mob_x_hbm,
    mob_y_hbm,
    mob_z_hbm,
    fraction_hbm,
    inverse_hbm,
    couplings_hbm,
    send_ref,
    recv_ref,
    near_row_ref,
    near_col_ref,
    out_x_hbm,
    out_r_hbm,
    res,
    mob_x,
    mob_y,
    mob_z,
    fraction,
    inverse,
    couplings,
    inv_diag,
    zed,
    direction,
    image,
    image_two,
    send_map,
    tile_table,
    back_table,
    low_mx,
    low_my,
    edge_my,
    edges,
    halo_x,
    halo_y,
    row_send,
    row_recv,
    link_send,
    link_recv,
    sum_send,
    sum_recv,
    load_sem,
    store_sem,
    side_send_sem,
    side_recv_sem,
    mob_send_sem,
    mob_recv_sem,
    row_send_sem,
    row_recv_sem,
    link_send_sem,
    link_recv_sem,
    sum_send_sem,
    sum_recv_sem,
):
    count_x, count_y = counts
    devices = count_x * count_y
    at_x, at_y = lax.axis_index("gx"), lax.axis_index("gy")
    me = at_x * count_y + at_y
    size_x, size_y, depth = res.shape
    tiles_z = depth // TZ
    group = 128 // (size_y * tiles_z)
    table_rows = size_x // group
    blocks = inverse.shape[0]
    push_count = near_row_ref.shape[1]
    unroll = 4

    loads = [
        pltpu.make_async_copy(src, dst, load_sem.at[n])
        for n, (src, dst) in enumerate(
            (
                (source_hbm, res),
                (fraction_hbm, fraction),
                (mob_y_hbm, mob_y),
                (mob_x_hbm, mob_x),
                (mob_z_hbm, mob_z),
                (inverse_hbm, inverse),
                (couplings_hbm, couplings),
            )
        )
    ]
    for load in loads:
        load.start()

    barrier = pltpu.get_barrier_semaphore()

    def peer(step):
        other = lax.rem(me + step, devices)
        return (other // count_y, lax.rem(other, count_y)), other

    def greet(step, carry):
        pl.semaphore_signal(barrier, inc=1, device_id=peer(step)[0], device_id_type=MESH)
        return carry

    low_mx[...] = jnp.zeros_like(low_mx)
    low_my[...] = jnp.zeros_like(low_my)
    halo_x[...] = jnp.zeros_like(halo_x)
    halo_y[...] = jnp.zeros_like(halo_y)
    lax.fori_loop(1, devices, greet, 0)

    def exchange(send, recv, send_sem, recv_sem, same=False):
        def one(step, carry):
            device, other = peer(step)
            pltpu.make_async_remote_copy(
                src_ref=send.at[0 if same else other],
                dst_ref=recv.at[me],
                send_sem=send_sem,
                recv_sem=recv_sem,
                device_id=device,
                device_id_type=MESH,
            ).start()
            return carry

        lax.fori_loop(1, devices, one, 0)
        recv[me] = send[0 if same else me]

    def arrived(recv, recv_sem):
        part = recv.at[pl.ds(0, devices - 1)]
        pltpu.make_async_copy(part, part, recv_sem).wait()

    tile = send_ref[...]
    low = tile & 127
    tile_k = low & (tiles_z - 1)
    tile_j = (low >> log2(tiles_z)) & (size_y - 1)
    tile_g = low >> log2(tiles_z * size_y)
    send_map[...] = (
        (tile - low) + tile_k * (group * size_y) + tile_g * size_y + tile_j
    )

    def stack_tiles(planes):
        return jnp.concatenate(
            [plane[:, k * TZ : (k + 1) * TZ] for k in range(tiles_z) for plane in planes],
            axis=0,
        )

    def total_tiles(alpha):
        def step(row, carry):
            planes = []
            for g in range(group):
                x = row * group + g
                plane = res[x]
                if alpha is not None:
                    plane = plane - alpha * image[x]
                    res[x] = plane
                planes.append(fraction[x] * plane)
            stacked = stack_tiles(planes)
            tile_table[pl.ds(row, 1), :] = jnp.sum(stacked.T, axis=0, keepdims=True)
            return carry

        lax.fori_loop(0, table_rows, step, 0)

    def coarse_send(phase, alpha):
        total_tiles(alpha)
        gather_rows(tile_table[...], send_map, row_send.at[2 * phase], unroll)

    def row_exchange(n):
        exchange(row_send.at[n], row_recv.at[n], row_send_sem.at[n], row_recv_sem.at[n])

    loads[0].wait()
    loads[1].wait()
    coarse_send(0, None)
    pl.semaphore_wait(barrier, devices - 1)
    row_exchange(0)

    near_row, near_col = near_row_ref[...], near_col_ref[...]
    target_row = near_row >> log2(blocks)
    target_col = near_col >> log2(blocks)
    earlier = iota((push_count, push_count), 0) < iota((push_count, push_count), 1)
    same = jnp.where((target_row == target_col) & earlier, 1, 0)
    rank = jnp.sum(same, axis=0, keepdims=True)
    slot = target_row * SLOT + rank
    chosen = iota((devices * SLOT, push_count), 0) == slot
    local = (near_row & (blocks - 1)).astype(F32)
    identity = jnp.sum(jnp.where(chosen, local, 0.0), axis=1, keepdims=True)
    link_send[0] = jnp.broadcast_to(identity, (devices * SLOT, 128)).reshape(
        devices, SLOT, 128
    )
    spread = jnp.where(chosen, 1.0, 0.0).astype(BF16)

    def link_exchange(n):
        exchange(link_send.at[n], link_recv.at[n], link_send_sem.at[n], link_recv_sem.at[n])

    link_exchange(0)

    def side_copy(src, dst, send_sem, recv_sem, shift_x, shift_y):
        return pltpu.make_async_remote_copy(
            src_ref=src,
            dst_ref=dst,
            send_sem=send_sem,
            recv_sem=recv_sem,
            device_id=(at_x + shift_x, at_y + shift_y),
            device_id_type=MESH,
        )

    loads[2].wait()
    loads[3].wait()

    def take_edge(x, carry):
        edge_my[x] = mob_y[x, size_y - 1 : size_y, :]
        return carry

    lax.fori_loop(0, size_x, take_edge, 0)
    copy_mx = side_copy(
        mob_x.at[size_x - 1], low_mx, mob_send_sem.at[0], mob_recv_sem.at[0], 1, 0
    )
    copy_my = side_copy(edge_my, low_my, mob_send_sem.at[1], mob_recv_sem.at[1], 0, 1)
    has_low_x, has_high_x = at_x > 0, at_x < count_x - 1
    has_low_y, has_high_y = at_y > 0, at_y < count_y - 1
    pl.when(has_high_x)(copy_mx.start)
    pl.when(has_high_y)(copy_my.start)

    lane = iota((size_y, depth), 1)
    row_of = iota((size_y, depth), 0)

    def below_z(plane):
        return jnp.where(lane == 0, 0.0, pltpu.roll(plane, 1, 1))

    def above_z(plane):
        return jnp.where(lane == depth - 1, 0.0, pltpu.roll(plane, depth - 1, 1))

    def below_y(plane, edge):
        return jnp.where(row_of == 0, edge, pltpu.roll(plane, 1, 0))

    def above_y(plane, edge):
        return jnp.where(row_of == size_y - 1, edge, pltpu.roll(plane, size_y - 1, 0))

    loads[4].wait()
    pl.when(has_low_x)(copy_mx.wait_recv)
    pl.when(has_low_y)(copy_my.wait_recv)

    def make_diagonal(x, lower):
        here = mob_x[x]
        mob_b, mob_c = mob_y[x], mob_z[x]
        value = (
            (here + lower)
            + (mob_b + below_y(mob_b, low_my[x]))
            + (mob_c + below_z(mob_c))
        )
        inv_diag[x] = 1.0 / value
        return here

    lax.fori_loop(0, size_x, make_diagonal, low_mx[...])

    def halo_copies(phase):
        out = []
        for side, (there, send, recv_here, shift_x, shift_y, came) in enumerate(
            (
                (has_low_x, 0, 1, -1, 0, has_high_x),
                (has_high_x, 1, 0, 1, 0, has_low_x),
                (has_low_y, 2, 1, 0, -1, has_high_y),
                (has_high_y, 3, 0, 0, 1, has_low_y),
            )
        ):
            field = zed if phase else direction
            if side < 2:
                src = field.at[0 if side == 0 else size_x - 1]
                dst = halo_x.at[phase, recv_here]
            else:
                src = edges.at[phase, side - 2]
                dst = halo_y.at[phase, recv_here]
            copy = side_copy(
                src,
                dst,
                side_send_sem.at[phase, side],
                side_recv_sem.at[phase, side],
                shift_x,
                shift_y,
            )
            out.append((there, came, copy))
        return out

    zero_plane = jnp.zeros((size_y, depth), F32)

    def precondition(phase):
        first, second = 2 * phase, 2 * phase + 1
        field = zed if phase else direction
        arrived(row_recv.at[first], row_recv_sem.at[first])
        totals = scatter_rows(row_recv.at[first], recv_ref, blocks, unroll)
        if phase == 0:
            loads[5].wait()
            loads[6].wait()
        sweep_one = block_products(totals, lambda p: inverse[p], blocks, 1)
        per_block = push_count // blocks
        pushed = block_products(sweep_one, lambda p: couplings[p], push_count, per_block)
        parts = split_three(pushed)
        out_values = jnp.zeros((devices * SLOT, 128), F32)
        for n in range(3):
            out_values = out_values + lax.dot_general(
                spread,
                parts[n * push_count : (n + 1) * push_count],
                NN,
                preferred_element_type=F32,
            )
        link_send[1 + phase] = out_values.reshape(devices, SLOT, 128)
        link_exchange(1 + phase)
        if phase == 0:
            arrived(link_recv.at[0], link_recv_sem.at[0])
        names = link_recv[0].reshape(devices * SLOT, 128).T[:blocks]
        gather_in = jnp.where(
            names == iota((blocks, devices * SLOT), 0).astype(F32), 1.0, 0.0
        ).astype(BF16)
        arrived(link_recv.at[1 + phase], link_recv_sem.at[1 + phase])
        values = split_three(link_recv[1 + phase].reshape(devices * SLOT, 128), axis=1)
        summed = lax.dot_general(gather_in, values, NN, preferred_element_type=F32)
        coupled = summed[:, :128] + summed[:, 128:256] + summed[:, 256:]
        sweep_two = block_products(totals - coupled, lambda p: inverse[p], blocks, 1)
        gather_rows(sweep_two, recv_ref, row_send.at[second], unroll)
        row_exchange(second)
        arrived(row_recv.at[second], row_recv_sem.at[second])
        back_table[...] = scatter_rows(row_recv.at[second], send_map, table_rows, unroll)

        def step(row, total):
            stacked = jnp.broadcast_to(back_table[pl.ds(row, 1), :], (128, 128)).T
            for g in range(group):
                x = row * group + g
                tiles = [
                    stacked[(k * group + g) * size_y : (k * group + g + 1) * size_y]
                    for k in range(tiles_z)
                ]
                here = res[x]
                value = fraction[x] * jnp.concatenate(tiles, axis=1) + here * inv_diag[x]
                field[x] = value
                edges[phase, 0, x] = value[0:1]
                edges[phase, 1, x] = value[size_y - 1 : size_y]
                total = total + here * value
            return total

        return jnp.sum(lax.fori_loop(0, table_rows, step, zero_plane))

    def apply_operator(phase, copies):
        field = zed if phase else direction
        result = image_two if phase else image
        for there, came, copy in copies:
            pl.when(there)(copy.start)
        for there, came, copy in copies:
            pl.when(came)(copy.wait_recv)

        def plane_step(x, below, here, above, lower):
            mob_a, mob_b, mob_c = mob_x[x], mob_y[x], mob_z[x]
            edge_low, edge_high = halo_y[phase, 0, x], halo_y[phase, 1, x]
            part_x = mob_a * (above - here) - lower * (here - below)
            part_y = mob_b * (above_y(here, edge_high) - here) - below_y(
                mob_b, low_my[x]
            ) * (here - below_y(here, edge_low))
            flux = mob_c * (above_z(here) - here)
            value = -(part_x + part_y + (flux - below_z(flux)))
            result[x] = value
            cross = value if phase == 0 else image[x]
            return here * value, here * cross, mob_a

        def step(x, carry):
            below, here, lower, total, cross = carry
            above = field[x + 1]
            one, two, lower = plane_step(x, below, here, above, lower)
            return here, above, lower, total + one, cross + two

        below, here, lower, total, cross = lax.fori_loop(
            0,
            size_x - 1,
            step,
            (halo_x[phase, 0], field[0], low_mx[...], zero_plane, zero_plane),
        )
        one, two, lower = plane_step(size_x - 1, below, here, halo_x[phase, 1], lower)
        return jnp.sum(total + one), jnp.sum(cross + two)

    def all_sums(phase, values):
        place = iota((1, 128), 1)
        row = jnp.zeros((1, 128), F32)
        for n, value in enumerate(values):
            row = jnp.where(place == n, value, row)
        sum_send[phase, 0] = row
        exchange(
            sum_send.at[phase],
            sum_recv.at[phase],
            sum_send_sem.at[phase],
            sum_recv_sem.at[phase],
            same=True,
        )
        arrived(sum_recv.at[phase], sum_recv_sem.at[phase])
        total = jnp.zeros((1, 128), F32)
        total = lax.fori_loop(
            0, devices, lambda n, total: total + sum_recv[phase, n], total
        )
        return [
            jnp.sum(jnp.where(place == n, total, 0.0), axis=1, keepdims=True)
            for n in range(len(values))
        ]

    copies_0, copies_1 = halo_copies(0), halo_copies(1)
    rz_part = precondition(0)
    energy_part, _ = apply_operator(0, copies_0)
    rz, energy = all_sums(0, (rz_part, energy_part))
    alpha = rz / energy

    coarse_send(1, alpha)
    row_exchange(2)
    next_part = precondition(1)
    own_part, cross_part = apply_operator(1, copies_1)
    rz_next, own, cross = all_sums(1, (next_part, own_part, cross_part))
    beta = rz_next / rz
    alpha_two = rz_next / (own + beta * (2.0 * cross + beta * energy))

    def finish(x, carry):
        first = direction[x]
        zed[x] = alpha * first + alpha_two * (zed[x] + beta * first)
        res[x] = res[x] - alpha_two * (image_two[x] + beta * image[x])
        return carry

    pl.when(has_high_x)(copy_mx.wait_send)
    pl.when(has_high_y)(copy_my.wait_send)
    for there, came, copy in copies_0 + copies_1:
        pl.when(there)(copy.wait_send)
    lax.fori_loop(0, size_x, finish, 0)
    stores = (
        pltpu.make_async_copy(zed, out_x_hbm, store_sem.at[0]),
        pltpu.make_async_copy(res, out_r_hbm, store_sem.at[1]),
    )
    for store in stores:
        store.start()
    for n in range(4):
        arrived(row_send.at[n], row_send_sem.at[n])
    for n in range(3):
        arrived(link_send.at[n], link_send_sem.at[n])
    for n in range(2):
        arrived(sum_recv.at[n], sum_send_sem.at[n])
    for store in stores:
        store.wait()


def body(
    source_term,
    mobility_x,
    mobility_y,
    mobility_z,
    bubble_fraction,
    tile_labels,
    send_tiles,
    recv_rows,
    block_inverse,
    couplings,
    neighbours,
):
    count_x, count_y = lax.axis_size("gx"), lax.axis_size("gy")
    devices = count_x * count_y
    size_x, size_y, depth = source_term.shape
    tiles = size_x * size_y * (depth // TZ)
    blocks, order = block_inverse.shape[:2]
    send, recv = send_tiles[0], recv_rows[0]
    pad = 128 - send.shape[1]
    assert order == 128 and pad >= 0
    if pad:
        send = jnp.pad(send, ((0, 0), (0, pad)), constant_values=tiles)
        recv = jnp.pad(recv, ((0, 0), (0, pad)), constant_values=blocks * order)
    push_count = neighbours.size
    table_rows = tiles // 128
    field = (size_x, size_y, depth)
    hbm = pl.BlockSpec(memory_space=pl.ANY)
    vmem = pl.BlockSpec(memory_space=pltpu.VMEM)
    dma = pltpu.SemaphoreType.DMA
    return pl.pallas_call(
        functools.partial(kernel, (count_x, count_y)),
        out_shape=(
            jax.ShapeDtypeStruct(field, F32),
            jax.ShapeDtypeStruct(field, F32),
        ),
        in_specs=[hbm] * 7 + [vmem] * 4,
        out_specs=(hbm, hbm),
        scratch_shapes=[
            pltpu.VMEM(field, F32),
            pltpu.VMEM(field, F32),
            pltpu.VMEM(field, F32),
            pltpu.VMEM(field, F32),
            pltpu.VMEM(field, F32),
            pltpu.VMEM((blocks, order, order), F32),
            pltpu.VMEM((push_count, order, order), F32),
            pltpu.VMEM(field, F32),
            pltpu.VMEM(field, F32),
            pltpu.VMEM(field, F32),
            pltpu.VMEM(field, F32),
            pltpu.VMEM(field, F32),
            pltpu.VMEM((devices, 128), jnp.int32),
            pltpu.VMEM((table_rows, 128), F32),
            pltpu.VMEM((table_rows, 128), F32),
            pltpu.VMEM((size_y, depth), F32),
            pltpu.VMEM((size_x, 1, depth), F32),
            pltpu.VMEM((size_x, 1, depth), F32),
            pltpu.VMEM((2, 2, size_x, 1, depth), F32),
            pltpu.VMEM((2, 2, size_y, depth), F32),
            pltpu.VMEM((2, 2, size_x, 1, depth), F32),
            pltpu.VMEM((4, devices, 1, 128), F32),
            pltpu.VMEM((4, devices, 1, 128), F32),
            pltpu.VMEM((3, devices, SLOT, 128), F32),
            pltpu.VMEM((3, devices, SLOT, 128), F32),
            pltpu.VMEM((2, 1, 1, 128), F32),
            pltpu.VMEM((2, devices, 1, 128), F32),
            dma((7,)),
            dma((2,)),
            dma((2, 4)),
            dma((2, 4)),
            dma((2,)),
            dma((2,)),
            dma((4,)),
            dma((4,)),
            dma((3,)),
            dma((3,)),
            dma((2,)),
            dma((2,)),
        ],
        compiler_params=pltpu.CompilerParams(
            collective_id=0, has_side_effects=True, vmem_limit_bytes=48 * 1024 * 1024
        ),
    )(
        source_term,
        mobility_x,
        mobility_y,
        mobility_z,
        bubble_fraction,
        block_inverse,
        couplings.reshape(push_count, order, order),
        send,
        recv,
        neighbours.reshape(1, push_count),
        neighbours.reshape(push_count, 1),
    )


def solution(mesh):
    return jax.shard_map(
        body,
        mesh=mesh,
        in_specs=(
            P("gx", "gy", None),
            P("gx", "gy", None),
            P("gx", "gy", None),
            P("gx", "gy", None),
            P("gx", "gy", None),
            P("gx", "gy", None),
            P(("gx", "gy"), None, None),
            P(("gx", "gy"), None, None),
            P(("gx", "gy"), None, None),
            P(("gx", "gy"), None, None, None),
            P(("gx", "gy"), None),
        ),
        out_specs=(P("gx", "gy", None), P("gx", "gy", None)),
        check_vma=False,
    )
```

```python
import functools

import jax
import jax.numpy as jnp
from jax import lax
from jax.experimental import pallas as pl
from jax.experimental.pallas import tpu as pltpu
from jax.sharding import PartitionSpec as P

TZ = 128
LINK = 4
SLOT = 8
F32 = jnp.float32
BF16 = jnp.bfloat16
MESH = pl.DeviceIdType.MESH
NT = (((1,), (1,)), ((), ()))
NN = (((1,), (0,)), ((), ()))
GROUP = 8


def log2(value):
    assert value & (value - 1) == 0
    return value.bit_length() - 1


def iota(shape, axis):
    return lax.broadcasted_iota(jnp.int32, shape, axis)


def split_two(value):
    first = value.astype(BF16).astype(F32)
    return first, (value - first).astype(BF16).astype(F32)


def stack_two(value, axis=0):
    return jnp.concatenate(split_two(value), axis=axis).astype(BF16)


def fold_two(value):
    half = value.shape[0] // 2
    return value[:half] + value[half:]


def fold_tiles(value):
    tiles = [
        value[y : y + 8, z : z + 128]
        for y in range(0, value.shape[0], 8)
        for z in range(0, value.shape[1], 128)
    ]
    while len(tiles) > 1:
        tiles = [a + b for a, b in zip(tiles[::2], tiles[1::2])]
    return tiles[0]


def write_one_hots(index_ref, hot_ref):
    def step(block, carry):
        for sub in range(GROUP):
            index = index_ref[pl.ds(block * GROUP + sub, 1), :]
            hot = jnp.where(iota((128, 128), 0) == (index & 127), 1.0, 0.0)
            hot_ref[block, :, sub * 128 : (sub + 1) * 128] = hot.astype(BF16)
        return carry

    lax.fori_loop(0, hot_ref.shape[0], step, 0)


def gather_rows(table, index_ref, hot_ref, out_ref):
    parts = stack_two(table)
    high_count = table.shape[0]

    def step(block, carry):
        picked = fold_two(
            lax.dot_general(parts, hot_ref[block], NN, preferred_element_type=F32)
        )
        for sub in range(GROUP):
            row = block * GROUP + sub
            hit = iota((high_count, 128), 0) == (index_ref[pl.ds(row, 1), :] >> 7)
            mine = picked[:, sub * 128 : (sub + 1) * 128]
            out_ref[row] = jnp.sum(jnp.where(hit, mine, 0.0), axis=0, keepdims=True)
        return carry

    lax.fori_loop(0, hot_ref.shape[0], step, 0)


def scatter_rows(value_ref, index_ref, hot_ref, high_count):
    def step(block, total):
        pieces = []
        for sub in range(GROUP):
            row = block * GROUP + sub
            hit = iota((high_count, 128), 0) == (index_ref[pl.ds(row, 1), :] >> 7)
            pieces.append(stack_two(jnp.where(hit, value_ref[row], 0.0)))
        return total + lax.dot_general(
            jnp.concatenate(pieces, axis=1), hot_ref[block], NT, preferred_element_type=F32
        )

    start = jnp.zeros((2 * high_count, 128), F32)
    return fold_two(lax.fori_loop(0, hot_ref.shape[0], step, start))


def block_vectors(vectors):
    first, second = split_two(vectors)
    out = []
    for q in range(vectors.shape[0]):
        mine = iota(vectors.shape, 0) == q
        top = jnp.where(mine, first, 0.0)
        low = jnp.where(mine, second, 0.0)
        upper = jnp.concatenate([top, top], axis=1)
        lower = jnp.concatenate([low, jnp.zeros_like(low)], axis=1)
        out.append(jnp.concatenate([upper, lower], axis=0).astype(BF16))
    return out


def block_products(vectors, split_ref):
    total = None
    for q, part in enumerate(block_vectors(vectors)):
        term = lax.dot_general(part, split_ref[q], NT, preferred_element_type=F32)
        total = term if total is None else total + term
    return fold_two(total)


def kernel(
    counts,
    source_hbm,
    mob_x_hbm,
    mob_y_hbm,
    mob_z_hbm,
    fraction_hbm,
    inverse_hbm,
    couplings_hbm,
    send_ref,
    recv_ref,
    near_row_ref,
    near_col_ref,
    out_x_hbm,
    out_r_hbm,
    res,
    mob_x,
    mob_y,
    mob_z,
    fraction,
    inverse,
    couplings,
    inv_diag,
    zed,
    direction,
    image,
    image_two,
    low_y,
    inverse_split,
    couplings_split,
    send_hot,
    recv_hot,
    send_map,
    tile_table,
    back_table,
    low_mx,
    low_my,
    edge_my,
    edges,
    halo_x,
    halo_y,
    row_send,
    row_recv,
    link_send,
    link_recv,
    sum_send,
    sum_recv,
    load_sem,
    store_sem,
    side_send_sem,
    side_recv_sem,
    mob_send_sem,
    mob_recv_sem,
    row_send_sem,
    row_recv_sem,
    link_send_sem,
    link_recv_sem,
    sum_send_sem,
    sum_recv_sem,
):
    count_x, count_y = counts
    devices = count_x * count_y
    at_x, at_y = lax.axis_index("gx"), lax.axis_index("gy")
    me = at_x * count_y + at_y
    size_x, size_y, depth = res.shape
    tiles_z = depth // TZ
    group = 128 // (size_y * tiles_z)
    table_rows = size_x // group
    blocks = inverse.shape[0]
    push_count = near_row_ref.shape[1]

    loads = [
        pltpu.make_async_copy(src, dst, load_sem.at[n])
        for n, (src, dst) in enumerate(
            (
                (source_hbm, res),
                (fraction_hbm, fraction),
                (mob_y_hbm, mob_y),
                (mob_x_hbm, mob_x),
                (mob_z_hbm, mob_z),
                (inverse_hbm, inverse),
                (couplings_hbm, couplings),
            )
        )
    ]
    for load in loads:
        load.start()

    barrier = pltpu.get_barrier_semaphore()

    def peer(step):
        other = lax.rem(me + step, devices)
        return (other // count_y, lax.rem(other, count_y)), other

    def greet(step, carry):
        pl.semaphore_signal(barrier, inc=1, device_id=peer(step)[0], device_id_type=MESH)
        return carry

    low_mx[...] = jnp.zeros_like(low_mx)
    low_my[...] = jnp.zeros_like(low_my)
    halo_x[...] = jnp.zeros_like(halo_x)
    halo_y[...] = jnp.zeros_like(halo_y)
    lax.fori_loop(1, devices, greet, 0)

    def exchange(send, recv, send_sem, recv_sem, same=False):
        def one(step, carry):
            device, other = peer(step)
            pltpu.make_async_remote_copy(
                src_ref=send.at[0 if same else other],
                dst_ref=recv.at[me],
                send_sem=send_sem,
                recv_sem=recv_sem,
                device_id=device,
                device_id_type=MESH,
            ).start()
            return carry

        lax.fori_loop(1, devices, one, 0)
        recv[me] = send[0 if same else me]

    def arrived(recv, recv_sem):
        part = recv.at[pl.ds(0, devices - 1)]
        pltpu.make_async_copy(part, part, recv_sem).wait()

    tile = send_ref[...]
    low = tile & 127
    tile_k = low & (tiles_z - 1)
    tile_j = (low >> log2(tiles_z)) & (size_y - 1)
    tile_g = low >> log2(tiles_z * size_y)
    send_map[...] = (
        (tile - low) + tile_k * (group * size_y) + tile_g * size_y + tile_j
    )

    def stack_tiles(planes):
        return jnp.concatenate(
            [plane[:, k * TZ : (k + 1) * TZ] for k in range(tiles_z) for plane in planes],
            axis=0,
        )

    def total_tiles(alpha):
        def step(row, carry):
            planes = []
            for g in range(group):
                x = row * group + g
                plane = res[x]
                if alpha is not None:
                    plane = plane - alpha * image[x]
                    res[x] = plane
                planes.append(fraction[x] * plane)
            stacked = stack_tiles(planes)
            tile_table[pl.ds(row, 1), :] = jnp.sum(stacked.T, axis=0, keepdims=True)
            return carry

        lax.fori_loop(0, table_rows, step, 0)

    def coarse_send(phase, alpha):
        total_tiles(alpha)
        gather_rows(tile_table[...], send_map, send_hot, row_send.at[2 * phase])

    def row_exchange(n):
        exchange(row_send.at[n], row_recv.at[n], row_send_sem.at[n], row_recv_sem.at[n])

    write_one_hots(send_map, send_hot)
    loads[0].wait()
    loads[1].wait()
    coarse_send(0, None)
    pl.semaphore_wait(barrier, devices - 1)
    row_exchange(0)

    near_row, near_col = near_row_ref[...], near_col_ref[...]
    target_row = near_row >> log2(blocks)
    target_col = near_col >> log2(blocks)
    earlier = iota((push_count, push_count), 0) < iota((push_count, push_count), 1)
    same = jnp.where((target_row == target_col) & earlier, 1, 0)
    rank = jnp.sum(same, axis=0, keepdims=True)
    slot = target_row * SLOT + rank
    chosen = iota((devices * SLOT, push_count), 0) == slot
    local = (near_row & (blocks - 1)).astype(F32)
    identity = jnp.sum(jnp.where(chosen, local, 0.0), axis=1, keepdims=True)
    link_send[0] = jnp.broadcast_to(identity, (devices * SLOT, 128)).reshape(
        devices, SLOT, 128
    )
    spread = jnp.where(chosen, 1.0, 0.0).astype(BF16)

    def link_exchange(n):
        exchange(link_send.at[n], link_recv.at[n], link_send_sem.at[n], link_recv_sem.at[n])

    link_exchange(0)

    def side_copy(src, dst, send_sem, recv_sem, shift_x, shift_y):
        return pltpu.make_async_remote_copy(
            src_ref=src,
            dst_ref=dst,
            send_sem=send_sem,
            recv_sem=recv_sem,
            device_id=(at_x + shift_x, at_y + shift_y),
            device_id_type=MESH,
        )

    loads[2].wait()
    loads[3].wait()

    def take_edge(x, carry):
        edge_my[x] = mob_y[x, size_y - 1 : size_y, :]
        return carry

    lax.fori_loop(0, size_x, take_edge, 0)
    copy_mx = side_copy(
        mob_x.at[size_x - 1], low_mx, mob_send_sem.at[0], mob_recv_sem.at[0], 1, 0
    )
    copy_my = side_copy(edge_my, low_my, mob_send_sem.at[1], mob_recv_sem.at[1], 0, 1)
    has_low_x, has_high_x = at_x > 0, at_x < count_x - 1
    has_low_y, has_high_y = at_y > 0, at_y < count_y - 1
    pl.when(has_high_x)(copy_mx.start)
    pl.when(has_high_y)(copy_my.start)

    lane = iota((size_y, depth), 1)
    row_of = iota((size_y, depth), 0)

    def below_z(plane):
        return jnp.where(lane == 0, 0.0, pltpu.roll(plane, 1, 1))

    def above_z(plane):
        return jnp.where(lane == depth - 1, 0.0, pltpu.roll(plane, depth - 1, 1))

    def below_y(plane, edge):
        return jnp.where(row_of == 0, edge, pltpu.roll(plane, 1, 0))

    def above_y(plane, edge):
        return jnp.where(row_of == size_y - 1, edge, pltpu.roll(plane, size_y - 1, 0))

    write_one_hots(recv_ref, recv_hot)
    loads[5].wait()

    def split_inverse(q, carry):
        inverse_split[q] = stack_two(inverse[q], axis=1)
        return carry

    lax.fori_loop(0, blocks, split_inverse, 0)
    loads[6].wait()

    def split_couplings(q, carry):
        couplings_split[q] = stack_two(
            jnp.concatenate([couplings[q, k] for k in range(couplings.shape[1])], axis=0),
            axis=1,
        )
        return carry

    lax.fori_loop(0, blocks, split_couplings, 0)

    def make_diagonal(x, lower):
        here = mob_x[x]
        mob_b, mob_c = mob_y[x], mob_z[x]
        lower_b = below_y(mob_b, low_my[x])
        low_y[x] = lower_b
        value = (here + lower) + (mob_b + lower_b) + (mob_c + below_z(mob_c))
        inv_diag[x] = 1.0 / value
        return here

    def halo_copies(phase):
        out = []
        for side, (there, send, recv_here, shift_x, shift_y, came) in enumerate(
            (
                (has_low_x, 0, 1, -1, 0, has_high_x),
                (has_high_x, 1, 0, 1, 0, has_low_x),
                (has_low_y, 2, 1, 0, -1, has_high_y),
                (has_high_y, 3, 0, 0, 1, has_low_y),
            )
        ):
            field = zed if phase else direction
            if side < 2:
                src = field.at[0 if side == 0 else size_x - 1]
                dst = halo_x.at[phase, recv_here]
            else:
                src = edges.at[phase, side - 2]
                dst = halo_y.at[phase, recv_here]
            copy = side_copy(
                src,
                dst,
                side_send_sem.at[phase, side],
                side_recv_sem.at[phase, side],
                shift_x,
                shift_y,
            )
            out.append((there, came, copy))
        return out

    zero_tile = jnp.zeros((8, 128), F32)

    def precondition(phase):
        first, second = 2 * phase, 2 * phase + 1
        field = zed if phase else direction
        arrived(row_recv.at[first], row_recv_sem.at[first])
        totals = scatter_rows(row_recv.at[first], recv_ref, recv_hot, blocks)
        sweep_one = block_products(totals, inverse_split)
        both = block_products(sweep_one, couplings_split)
        pushed = jnp.concatenate(
            [both[:, k * 128 : (k + 1) * 128] for k in range(couplings.shape[1])], axis=0
        )
        upper, lower = split_two(pushed)
        out_values = lax.dot_general(
            spread, upper.astype(BF16), NN, preferred_element_type=F32
        ) + lax.dot_general(spread, lower.astype(BF16), NN, preferred_element_type=F32)
        link_send[1 + phase] = out_values.reshape(devices, SLOT, 128)
        link_exchange(1 + phase)
        if phase == 0:
            loads[4].wait()
            pl.when(has_low_x)(copy_mx.wait_recv)
            pl.when(has_low_y)(copy_my.wait_recv)
            lax.fori_loop(0, size_x, make_diagonal, low_mx[...])
            arrived(link_recv.at[0], link_recv_sem.at[0])
        names = link_recv[0].reshape(devices * SLOT, 128).T[:blocks]
        gather_in = jnp.where(
            names == iota((blocks, devices * SLOT), 0).astype(F32), 1.0, 0.0
        ).astype(BF16)
        arrived(link_recv.at[1 + phase], link_recv_sem.at[1 + phase])
        values = stack_two(link_recv[1 + phase].reshape(devices * SLOT, 128), axis=1)
        summed = lax.dot_general(gather_in, values, NN, preferred_element_type=F32)
        coupled = summed[:, :128] + summed[:, 128:]
        sweep_two = block_products(totals - coupled, inverse_split)
        gather_rows(sweep_two, recv_ref, recv_hot, row_send.at[second])
        row_exchange(second)
        arrived(row_recv.at[second], row_recv_sem.at[second])
        back_table[...] = scatter_rows(
            row_recv.at[second], send_map, send_hot, table_rows
        )

        def step(row, total):
            stacked = jnp.broadcast_to(back_table[pl.ds(row, 1), :], (128, 128)).T
            for g in range(group):
                x = row * group + g
                tiles = [
                    stacked[(k * group + g) * size_y : (k * group + g + 1) * size_y]
                    for k in range(tiles_z)
                ]
                here = res[x]
                value = fraction[x] * jnp.concatenate(tiles, axis=1) + here * inv_diag[x]
                field[x] = value
                edges[phase, 0, x] = value[0:1]
                edges[phase, 1, x] = value[size_y - 1 : size_y]
                total = total + fold_tiles(here * value)
            return total

        return jnp.sum(lax.fori_loop(0, table_rows, step, zero_tile))

    def apply_operator(phase, copies):
        field = zed if phase else direction
        result = image_two if phase else image
        for there, came, copy in copies:
            pl.when(there)(copy.start)
        for there, came, copy in copies:
            pl.when(came)(copy.wait_recv)

        def plane_step(x, below, here, above, lower):
            mob_a, mob_b, mob_c = mob_x[x], mob_y[x], mob_z[x]
            edge_low, edge_high = halo_y[phase, 0, x], halo_y[phase, 1, x]
            part_x = mob_a * (above - here) - lower * (here - below)
            part_y = mob_b * (above_y(here, edge_high) - here) - low_y[x] * (
                here - below_y(here, edge_low)
            )
            flux = mob_c * (above_z(here) - here)
            value = -(part_x + part_y + (flux - below_z(flux)))
            result[x] = value
            one = fold_tiles(here * value)
            return one, fold_tiles(here * image[x]) if phase else one, mob_a

        def step(x, carry):
            below, here, lower, total, cross = carry
            above = field[x + 1]
            one, two, lower = plane_step(x, below, here, above, lower)
            return here, above, lower, total + one, cross + two

        below, here, lower, total, cross = lax.fori_loop(
            0,
            size_x - 1,
            step,
            (halo_x[phase, 0], field[0], low_mx[...], zero_tile, zero_tile),
        )
        one, two, lower = plane_step(size_x - 1, below, here, halo_x[phase, 1], lower)
        return jnp.sum(total + one), jnp.sum(cross + two)

    def all_sums(phase, values):
        place = iota((1, 128), 1)
        row = jnp.zeros((1, 128), F32)
        for n, value in enumerate(values):
            row = jnp.where(place == n, value, row)
        sum_send[phase, 0] = row
        exchange(
            sum_send.at[phase],
            sum_recv.at[phase],
            sum_send_sem.at[phase],
            sum_recv_sem.at[phase],
            same=True,
        )
        arrived(sum_recv.at[phase], sum_recv_sem.at[phase])
        total = jnp.zeros((1, 128), F32)
        total = lax.fori_loop(
            0, devices, lambda n, total: total + sum_recv[phase, n], total
        )
        return [
            jnp.sum(jnp.where(place == n, total, 0.0), axis=1, keepdims=True)
            for n in range(len(values))
        ]

    copies_0, copies_1 = halo_copies(0), halo_copies(1)
    rz_part = precondition(0)
    energy_part, _ = apply_operator(0, copies_0)
    rz, energy = all_sums(0, (rz_part, energy_part))
    alpha = rz / energy

    coarse_send(1, alpha)
    row_exchange(2)
    next_part = precondition(1)
    own_part, cross_part = apply_operator(1, copies_1)
    rz_next, own, cross = all_sums(1, (next_part, own_part, cross_part))
    beta = rz_next / rz
    alpha_two = rz_next / (own + beta * (2.0 * cross + beta * energy))

    def finish(x, carry):
        first = direction[x]
        zed[x] = alpha * first + alpha_two * (zed[x] + beta * first)
        res[x] = res[x] - alpha_two * (image_two[x] + beta * image[x])
        return carry

    pl.when(has_high_x)(copy_mx.wait_send)
    pl.when(has_high_y)(copy_my.wait_send)
    for there, came, copy in copies_0 + copies_1:
        pl.when(there)(copy.wait_send)
    lax.fori_loop(0, size_x, finish, 0)
    stores = (
        pltpu.make_async_copy(zed, out_x_hbm, store_sem.at[0]),
        pltpu.make_async_copy(res, out_r_hbm, store_sem.at[1]),
    )
    for store in stores:
        store.start()
    for n in range(4):
        arrived(row_send.at[n], row_send_sem.at[n])
    for n in range(3):
        arrived(link_send.at[n], link_send_sem.at[n])
    for n in range(2):
        arrived(sum_recv.at[n], sum_send_sem.at[n])
    for store in stores:
        store.wait()


def body(
    source_term,
    mobility_x,
    mobility_y,
    mobility_z,
    bubble_fraction,
    tile_labels,
    send_tiles,
    recv_rows,
    block_inverse,
    couplings,
    neighbours,
):
    count_x, count_y = lax.axis_size("gx"), lax.axis_size("gy")
    devices = count_x * count_y
    size_x, size_y, depth = source_term.shape
    tiles = size_x * size_y * (depth // TZ)
    blocks, order = block_inverse.shape[:2]
    send, recv = send_tiles[0], recv_rows[0]
    pad = 128 - send.shape[1]
    assert order == 128 and pad >= 0
    if pad:
        send = jnp.pad(send, ((0, 0), (0, pad)), constant_values=tiles)
        recv = jnp.pad(recv, ((0, 0), (0, pad)), constant_values=blocks * order)
    push_count = neighbours.size
    table_rows = tiles // 128
    field = (size_x, size_y, depth)
    hbm = pl.BlockSpec(memory_space=pl.ANY)
    vmem = pl.BlockSpec(memory_space=pltpu.VMEM)
    dma = pltpu.SemaphoreType.DMA
    return pl.pallas_call(
        functools.partial(kernel, (count_x, count_y)),
        out_shape=(
            jax.ShapeDtypeStruct(field, F32),
            jax.ShapeDtypeStruct(field, F32),
        ),
        in_specs=[hbm] * 7 + [vmem] * 4,
        out_specs=(hbm, hbm),
        scratch_shapes=[
            pltpu.VMEM(field, F32),
            pltpu.VMEM(field, F32),
            pltpu.VMEM(field, F32),
            pltpu.VMEM(field, F32),
            pltpu.VMEM(field, F32),
            pltpu.VMEM((blocks, order, order), F32),
            pltpu.VMEM(couplings.shape, F32),
            pltpu.VMEM(field, F32),
            pltpu.VMEM(field, F32),
            pltpu.VMEM(field, F32),
            pltpu.VMEM(field, F32),
            pltpu.VMEM(field, F32),
            pltpu.VMEM(field, F32),
            pltpu.VMEM((blocks, order, 2 * order), BF16),
            pltpu.VMEM((blocks, order * couplings.shape[1], 2 * order), BF16),
            pltpu.VMEM((devices // GROUP, 128, GROUP * 128), BF16),
            pltpu.VMEM((devices // GROUP, 128, GROUP * 128), BF16),
            pltpu.VMEM((devices, 128), jnp.int32),
            pltpu.VMEM((table_rows, 128), F32),
            pltpu.VMEM((table_rows, 128), F32),
            pltpu.VMEM((size_y, depth), F32),
            pltpu.VMEM((size_x, 1, depth), F32),
            pltpu.VMEM((size_x, 1, depth), F32),
            pltpu.VMEM((2, 2, size_x, 1, depth), F32),
            pltpu.VMEM((2, 2, size_y, depth), F32),
            pltpu.VMEM((2, 2, size_x, 1, depth), F32),
            pltpu.VMEM((4, devices, 1, 128), F32),
            pltpu.VMEM((4, devices, 1, 128), F32),
            pltpu.VMEM((3, devices, SLOT, 128), F32),
            pltpu.VMEM((3, devices, SLOT, 128), F32),
            pltpu.VMEM((2, 1, 1, 128), F32),
            pltpu.VMEM((2, devices, 1, 128), F32),
            dma((7,)),
            dma((2,)),
            dma((2, 4)),
            dma((2, 4)),
            dma((2,)),
            dma((2,)),
            dma((4,)),
            dma((4,)),
            dma((3,)),
            dma((3,)),
            dma((2,)),
            dma((2,)),
        ],
        compiler_params=pltpu.CompilerParams(
            collective_id=0, has_side_effects=True, vmem_limit_bytes=63 * 1024 * 1024
        ),
    )(
        source_term,
        mobility_x,
        mobility_y,
        mobility_z,
        bubble_fraction,
        block_inverse,
        couplings,
        send,
        recv,
        neighbours.T.reshape(1, push_count),
        neighbours.T.reshape(push_count, 1),
    )


def solution(mesh):
    return jax.shard_map(
        body,
        mesh=mesh,
        in_specs=(
            P("gx", "gy", None),
            P("gx", "gy", None),
            P("gx", "gy", None),
            P("gx", "gy", None),
            P("gx", "gy", None),
            P("gx", "gy", None),
            P(("gx", "gy"), None, None),
            P(("gx", "gy"), None, None),
            P(("gx", "gy"), None, None),
            P(("gx", "gy"), None, None, None),
            P(("gx", "gy"), None),
        ),
        out_specs=(P("gx", "gy", None), P("gx", "gy", None)),
        check_vma=False,
    )
```

```python
import functools

import jax
import jax.numpy as jnp
from jax import lax
from jax.experimental import pallas as pl
from jax.experimental.pallas import tpu as pltpu
from jax.sharding import PartitionSpec as P

TZ = 128
LINK = 4
SLOT = 4
F32 = jnp.float32
BF16 = jnp.bfloat16
MESH = pl.DeviceIdType.MESH
NT = (((1,), (1,)), ((), ()))
NN = (((1,), (0,)), ((), ()))
GROUP = 8


def log2(value):
    assert value & (value - 1) == 0
    return value.bit_length() - 1


def iota(shape, axis):
    return lax.broadcasted_iota(jnp.int32, shape, axis)


def split_two(value):
    first = value.astype(BF16).astype(F32)
    return first, (value - first).astype(BF16).astype(F32)


def stack_two(value, axis=0):
    return jnp.concatenate(split_two(value), axis=axis).astype(BF16)


def fold_two(value):
    half = value.shape[0] // 2
    return value[:half] + value[half:]


def fold_tiles(value):
    tiles = [
        value[y : y + 8, z : z + 128]
        for y in range(0, value.shape[0], 8)
        for z in range(0, value.shape[1], 128)
    ]
    while len(tiles) > 1:
        tiles = [a + b for a, b in zip(tiles[::2], tiles[1::2])]
    return tiles[0]


def write_one_hots(index_ref, hot_ref):
    def step(block, carry):
        for sub in range(GROUP):
            index = index_ref[pl.ds(block * GROUP + sub, 1), :]
            hot = jnp.where(iota((128, 128), 0) == (index & 127), 1.0, 0.0)
            hot_ref[block, :, sub * 128 : (sub + 1) * 128] = hot.astype(BF16)
        return carry

    lax.fori_loop(0, hot_ref.shape[0], step, 0)


def gather_rows(table, index_ref, hot_ref, out_ref):
    parts = stack_two(table)
    high_count = table.shape[0]

    def step(block, carry):
        picked = fold_two(
            lax.dot_general(parts, hot_ref[block], NN, preferred_element_type=F32)
        )
        for sub in range(GROUP):
            row = block * GROUP + sub
            hit = iota((high_count, 128), 0) == (index_ref[pl.ds(row, 1), :] >> 7)
            mine = picked[:, sub * 128 : (sub + 1) * 128]
            out_ref[row] = jnp.sum(jnp.where(hit, mine, 0.0), axis=0, keepdims=True)
        return carry

    lax.fori_loop(0, hot_ref.shape[0], step, 0)


def scatter_rows(value_ref, index_ref, hot_ref, high_count):
    def step(block, total):
        pieces = []
        for sub in range(GROUP):
            row = block * GROUP + sub
            hit = iota((high_count, 128), 0) == (index_ref[pl.ds(row, 1), :] >> 7)
            pieces.append(stack_two(jnp.where(hit, value_ref[row], 0.0)))
        return total + lax.dot_general(
            jnp.concatenate(pieces, axis=1), hot_ref[block], NT, preferred_element_type=F32
        )

    start = jnp.zeros((2 * high_count, 128), F32)
    return fold_two(lax.fori_loop(0, hot_ref.shape[0], step, start))


def block_vectors(vectors):
    first, second = split_two(vectors)
    out = []
    for q in range(vectors.shape[0]):
        mine = iota(vectors.shape, 0) == q
        top = jnp.where(mine, first, 0.0)
        low = jnp.where(mine, second, 0.0)
        upper = jnp.concatenate([top, top], axis=1)
        lower = jnp.concatenate([low, jnp.zeros_like(low)], axis=1)
        out.append(jnp.concatenate([upper, lower], axis=0).astype(BF16))
    return out


def block_products(vectors, split_ref):
    total = None
    for q, part in enumerate(block_vectors(vectors)):
        term = lax.dot_general(part, split_ref[q], NT, preferred_element_type=F32)
        total = term if total is None else total + term
    return fold_two(total)


def kernel(
    counts,
    source_hbm,
    mob_x_hbm,
    mob_y_hbm,
    mob_z_hbm,
    fraction_hbm,
    inverse_hbm,
    couplings_hbm,
    send_ref,
    recv_ref,
    near_ref,
    out_x,
    out_r,
    res,
    mob_x,
    mob_y,
    mob_z,
    fraction,
    inverse,
    couplings,
    inv_diag,
    zed,
    direction,
    image,
    image_two,
    low_y,
    inverse_split,
    couplings_split,
    send_hot,
    recv_hot,
    send_map,
    tile_table,
    back_table,
    low_mx,
    low_my,
    edge_my,
    edges,
    halo_x,
    halo_y,
    row_send,
    row_recv,
    link_send,
    link_recv,
    sum_send,
    sum_recv,
    load_sem,
    side_send_sem,
    side_recv_sem,
    mob_send_sem,
    mob_recv_sem,
    row_send_sem,
    row_recv_sem,
    link_send_sem,
    link_recv_sem,
    sum_send_sem,
    sum_recv_sem,
):
    count_x, count_y = counts
    devices = count_x * count_y
    at_x, at_y = lax.axis_index("gx"), lax.axis_index("gy")
    me = at_x * count_y + at_y
    size_x, size_y, depth = res.shape
    tiles_z = depth // TZ
    group = 128 // (size_y * tiles_z)
    table_rows = size_x // group
    blocks = inverse.shape[0]
    push_count = near_ref.size

    loads = [
        pltpu.make_async_copy(src, dst, load_sem.at[n])
        for n, (src, dst) in enumerate(
            (
                (source_hbm, res),
                (fraction_hbm, fraction),
                (mob_y_hbm, mob_y),
                (mob_x_hbm, mob_x),
                (mob_z_hbm, mob_z),
                (inverse_hbm, inverse),
                (couplings_hbm, couplings),
            )
        )
    ]
    for load in loads:
        load.start()

    barrier = pltpu.get_barrier_semaphore()

    def peer(step):
        other = lax.rem(me + step, devices)
        return (other // count_y, lax.rem(other, count_y)), other

    def greet(step, carry):
        pl.semaphore_signal(barrier, inc=1, device_id=peer(step)[0], device_id_type=MESH)
        return carry

    low_mx[...] = jnp.zeros_like(low_mx)
    low_my[...] = jnp.zeros_like(low_my)
    halo_x[...] = jnp.zeros_like(halo_x)
    halo_y[...] = jnp.zeros_like(halo_y)
    lax.fori_loop(1, devices, greet, 0)

    def exchange(send, recv, send_sem, recv_sem, same=False):
        def one(step, carry):
            device, other = peer(step)
            pltpu.make_async_remote_copy(
                src_ref=send.at[0 if same else other],
                dst_ref=recv.at[me],
                send_sem=send_sem,
                recv_sem=recv_sem,
                device_id=device,
                device_id_type=MESH,
            ).start()
            return carry

        lax.fori_loop(1, devices, one, 0)
        recv[me] = send[0 if same else me]

    def arrived(recv, recv_sem):
        part = recv.at[pl.ds(0, devices - 1)]
        pltpu.make_async_copy(part, part, recv_sem).wait()

    tile = send_ref[...]
    low = tile & 127
    tile_k = low & (tiles_z - 1)
    tile_j = (low >> log2(tiles_z)) & (size_y - 1)
    tile_g = low >> log2(tiles_z * size_y)
    send_map[...] = (
        (tile - low) + tile_k * (group * size_y) + tile_g * size_y + tile_j
    )

    def stack_tiles(planes):
        return jnp.concatenate(
            [plane[:, k * TZ : (k + 1) * TZ] for k in range(tiles_z) for plane in planes],
            axis=0,
        )

    def coarse_send(phase, field):
        def step(row, carry):
            planes = [fraction[x] * field[x] for x in [row * group + g for g in range(group)]]
            stacked = stack_tiles(planes)
            tile_table[pl.ds(row, 1), :] = jnp.sum(stacked.T, axis=0, keepdims=True)
            return carry

        lax.fori_loop(0, table_rows, step, 0)
        gather_rows(tile_table[...], send_map, send_hot, row_send.at[2 * phase])

    def row_exchange(n):
        exchange(row_send.at[n], row_recv.at[n], row_send_sem.at[n], row_recv_sem.at[n])

    write_one_hots(send_map, send_hot)
    loads[0].wait()
    loads[1].wait()
    coarse_send(0, res)
    pl.semaphore_wait(barrier, devices - 1)
    row_exchange(0)

    near_row = jnp.concatenate([near_ref[k : k + 1] for k in range(near_ref.shape[0])], axis=1)
    target_row = near_row >> log2(blocks)
    down, across = iota((push_count, push_count), 0), iota((push_count, push_count), 1)
    target_col = jnp.sum(
        jnp.where(down == across, target_row.astype(F32), 0.0), axis=1, keepdims=True
    ).astype(jnp.int32)
    earlier = down < across
    same = jnp.where((target_row == target_col) & earlier, 1, 0)
    rank = jnp.sum(same, axis=0, keepdims=True)
    slot = target_row * SLOT + rank
    chosen = iota((devices * SLOT, push_count), 0) == slot
    local = (near_row & (blocks - 1)).astype(F32)
    identity = jnp.sum(jnp.where(chosen, local, 0.0), axis=1, keepdims=True)
    link_send[0] = jnp.broadcast_to(identity, (devices * SLOT, 128)).reshape(
        devices, SLOT, 128
    )
    spread = jnp.where(chosen, 1.0, 0.0).astype(BF16)

    def link_exchange(n):
        exchange(link_send.at[n], link_recv.at[n], link_send_sem.at[n], link_recv_sem.at[n])

    link_exchange(0)

    def side_copy(src, dst, send_sem, recv_sem, shift_x, shift_y):
        return pltpu.make_async_remote_copy(
            src_ref=src,
            dst_ref=dst,
            send_sem=send_sem,
            recv_sem=recv_sem,
            device_id=(at_x + shift_x, at_y + shift_y),
            device_id_type=MESH,
        )

    loads[2].wait()
    loads[3].wait()

    def take_edge(x, carry):
        edge_my[x] = mob_y[x, size_y - 1 : size_y, :]
        return carry

    lax.fori_loop(0, size_x, take_edge, 0)
    copy_mx = side_copy(
        mob_x.at[size_x - 1], low_mx, mob_send_sem.at[0], mob_recv_sem.at[0], 1, 0
    )
    copy_my = side_copy(edge_my, low_my, mob_send_sem.at[1], mob_recv_sem.at[1], 0, 1)
    has_low_x, has_high_x = at_x > 0, at_x < count_x - 1
    has_low_y, has_high_y = at_y > 0, at_y < count_y - 1
    pl.when(has_high_x)(copy_mx.start)
    pl.when(has_high_y)(copy_my.start)

    lane = iota((size_y, depth), 1)
    row_of = iota((size_y, depth), 0)

    def below_z(plane):
        return jnp.where(lane == 0, 0.0, pltpu.roll(plane, 1, 1))

    def above_z(plane):
        return jnp.where(lane == depth - 1, 0.0, pltpu.roll(plane, depth - 1, 1))

    def below_y(plane, edge):
        return jnp.where(row_of == 0, edge, pltpu.roll(plane, 1, 0))

    def above_y(plane, edge):
        return jnp.where(row_of == size_y - 1, edge, pltpu.roll(plane, size_y - 1, 0))

    write_one_hots(recv_ref, recv_hot)
    loads[5].wait()

    def split_inverse(q, carry):
        inverse_split[q] = stack_two(inverse[q], axis=1)
        return carry

    lax.fori_loop(0, blocks, split_inverse, 0)
    loads[6].wait()

    def split_couplings(q, carry):
        couplings_split[q] = stack_two(
            jnp.concatenate([couplings[q, k] for k in range(couplings.shape[1])], axis=0),
            axis=1,
        )
        return carry

    lax.fori_loop(0, blocks, split_couplings, 0)

    def make_diagonal(x, lower):
        here = mob_x[x]
        mob_b, mob_c = mob_y[x], mob_z[x]
        lower_b = below_y(mob_b, low_my[x])
        low_y[x] = lower_b
        value = (here + lower) + (mob_b + lower_b) + (mob_c + below_z(mob_c))
        inv_diag[x] = 1.0 / value
        return here

    def halo_copies(phase):
        out = []
        for side, (there, send, recv_here, shift_x, shift_y, came) in enumerate(
            (
                (has_low_x, 0, 1, -1, 0, has_high_x),
                (has_high_x, 1, 0, 1, 0, has_low_x),
                (has_low_y, 2, 1, 0, -1, has_high_y),
                (has_high_y, 3, 0, 0, 1, has_low_y),
            )
        ):
            field = zed if phase else direction
            if side < 2:
                src = field.at[0 if side == 0 else size_x - 1]
                dst = halo_x.at[phase, recv_here]
            else:
                src = edges.at[phase, side - 2]
                dst = halo_y.at[phase, recv_here]
            copy = side_copy(
                src,
                dst,
                side_send_sem.at[phase, side],
                side_recv_sem.at[phase, side],
                shift_x,
                shift_y,
            )
            out.append((there, came, copy))
        return out

    zero_tile = jnp.zeros((8, 128), F32)

    def coarse_totals(phase):
        n = 2 * phase
        arrived(row_recv.at[n], row_recv_sem.at[n])
        return scatter_rows(row_recv.at[n], recv_ref, recv_hot, blocks)

    def precondition(phase, totals):
        second = 2 * phase + 1
        field = zed if phase else direction
        sweep_one = block_products(totals, inverse_split)
        both = block_products(sweep_one, couplings_split)
        pushed = jnp.concatenate(
            [both[:, k * 128 : (k + 1) * 128] for k in range(couplings.shape[1])], axis=0
        )
        upper, lower = split_two(pushed)
        out_values = lax.dot_general(
            spread, upper.astype(BF16), NN, preferred_element_type=F32
        ) + lax.dot_general(spread, lower.astype(BF16), NN, preferred_element_type=F32)
        link_send[1 + phase] = out_values.reshape(devices, SLOT, 128)
        link_exchange(1 + phase)
        if phase == 0:
            loads[4].wait()
            pl.when(has_low_x)(copy_mx.wait_recv)
            pl.when(has_low_y)(copy_my.wait_recv)
            lax.fori_loop(0, size_x, make_diagonal, low_mx[...])
            arrived(link_recv.at[0], link_recv_sem.at[0])
        names = link_recv[0].reshape(devices * SLOT, 128).T[:blocks]
        gather_in = jnp.where(
            names == iota((blocks, devices * SLOT), 0).astype(F32), 1.0, 0.0
        ).astype(BF16)
        arrived(link_recv.at[1 + phase], link_recv_sem.at[1 + phase])
        values = stack_two(link_recv[1 + phase].reshape(devices * SLOT, 128), axis=1)
        summed = lax.dot_general(gather_in, values, NN, preferred_element_type=F32)
        coupled = summed[:, :128] + summed[:, 128:]
        sweep_two = block_products(totals - coupled, inverse_split)
        gather_rows(sweep_two, recv_ref, recv_hot, row_send.at[second])
        row_exchange(second)
        arrived(row_recv.at[second], row_recv_sem.at[second])
        back_table[...] = scatter_rows(
            row_recv.at[second], send_map, send_hot, table_rows
        )

        def step(row, total):
            stacked = jnp.broadcast_to(back_table[pl.ds(row, 1), :], (128, 128)).T
            for g in range(group):
                x = row * group + g
                tiles = [
                    stacked[(k * group + g) * size_y : (k * group + g + 1) * size_y]
                    for k in range(tiles_z)
                ]
                here = res[x]
                value = fraction[x] * jnp.concatenate(tiles, axis=1) + here * inv_diag[x]
                field[x] = value
                edges[phase, 0, x] = value[0:1]
                edges[phase, 1, x] = value[size_y - 1 : size_y]
                total = total + fold_tiles(here * value)
            return total

        return jnp.sum(lax.fori_loop(0, table_rows, step, zero_tile))

    def apply_operator(phase, copies):
        field = zed if phase else direction
        result = image_two if phase else image
        for there, came, copy in copies:
            pl.when(there)(copy.start)
        def plane_step(x, below, here, above, lower):
            mob_a, mob_b, mob_c = mob_x[x], mob_y[x], mob_z[x]
            part_x = mob_a * (above - here) - lower * (here - below)
            part_y = mob_b * (above_y(here, 0.0) - here) - low_y[x] * (
                here - below_y(here, 0.0)
            )
            flux = mob_c * (above_z(here) - here)
            value = -(part_x + part_y + (flux - below_z(flux)))
            result[x] = value
            one = fold_tiles(here * value)
            return one, fold_tiles(here * image[x]) if phase else one, mob_a

        def step(x, carry):
            below, here, lower, total, cross = carry
            above = field[x + 1]
            one, two, lower = plane_step(x, below, here, above, lower)
            return here, above, lower, total + one, cross + two

        zero_plane = jnp.zeros((size_y, depth), F32)
        below, here, lower, total, cross = lax.fori_loop(
            0,
            size_x - 1,
            step,
            (zero_plane, field[0], low_mx[...], zero_tile, zero_tile),
        )
        one, two, lower = plane_step(size_x - 1, below, here, zero_plane, lower)
        total, cross = total + one, cross + two

        for there, came, copy in copies:
            pl.when(came)(copy.wait_recv)
        for x, weight, beside in (
            (0, low_mx[...], halo_x[phase, 0]),
            (size_x - 1, mob_x[size_x - 1], halo_x[phase, 1]),
        ):
            change = weight * beside
            result[x] = result[x] - change
            total = total - fold_tiles(field[x] * change)

        def edge_step(block, total):
            for sub in range(4):
                x = block * 4 + sub
                for y, weight, beside in (
                    (0, low_y, halo_y[phase, 0, x]),
                    (size_y - 1, mob_y, halo_y[phase, 1, x]),
                ):
                    change = weight[x, y : y + 1, :] * beside
                    result[x, y : y + 1, :] = result[x, y : y + 1, :] - change
                    total = total - field[x, y : y + 1, :] * change
            return total

        edge_total = lax.fori_loop(0, size_x // 4, edge_step, jnp.zeros((1, depth), F32))
        return jnp.sum(total) + jnp.sum(edge_total), jnp.sum(cross)

    place = iota((1, 128), 1)

    def start_sums(phase, values):
        row = jnp.zeros((1, 128), F32)
        for n, value in enumerate(values):
            row = jnp.where(place == n, value, row)
        sum_send[phase, 0] = row
        exchange(
            sum_send.at[phase],
            sum_recv.at[phase],
            sum_send_sem.at[phase],
            sum_recv_sem.at[phase],
            same=True,
        )

    def end_sums(phase, count):
        arrived(sum_recv.at[phase], sum_recv_sem.at[phase])
        totals = [sum_recv[phase, n] for n in range(4)]
        for n in range(4, devices):
            totals[n % 4] = totals[n % 4] + sum_recv[phase, n]
        total = (totals[0] + totals[1]) + (totals[2] + totals[3])
        return [
            jnp.sum(jnp.where(place == n, total, 0.0), axis=1, keepdims=True)
            for n in range(count)
        ]

    copies_0, copies_1 = halo_copies(0), halo_copies(1)
    totals = coarse_totals(0)
    rz_part = precondition(0, totals)
    energy_part, _ = apply_operator(0, copies_0)
    start_sums(0, (rz_part, energy_part))

    coarse_send(1, image)
    row_exchange(2)
    rz, energy = end_sums(0, 2)
    alpha = rz / energy

    def update_residual(x, carry):
        res[x] = res[x] - alpha * image[x]
        return carry

    lax.fori_loop(0, size_x, update_residual, 0)
    totals = totals - alpha * coarse_totals(1)
    next_part = precondition(1, totals)
    own_part, cross_part = apply_operator(1, copies_1)
    start_sums(1, (next_part, own_part, cross_part))
    rz_next, own, cross = end_sums(1, 3)
    beta = rz_next / rz
    alpha_two = rz_next / (own + beta * (2.0 * cross + beta * energy))

    def finish(x, carry):
        first = direction[x]
        out_x[x] = alpha * first + alpha_two * (zed[x] + beta * first)
        out_r[x] = res[x] - alpha_two * (image_two[x] + beta * image[x])
        return carry

    lax.fori_loop(0, size_x, finish, 0)
    pl.when(has_high_x)(copy_mx.wait_send)
    pl.when(has_high_y)(copy_my.wait_send)
    for there, came, copy in copies_0 + copies_1:
        pl.when(there)(copy.wait_send)
    for n in range(4):
        arrived(row_send.at[n], row_send_sem.at[n])
    for n in range(3):
        arrived(link_send.at[n], link_send_sem.at[n])
    for n in range(2):
        arrived(sum_recv.at[n], sum_send_sem.at[n])


def body(
    source_term,
    mobility_x,
    mobility_y,
    mobility_z,
    bubble_fraction,
    tile_labels,
    send_tiles,
    recv_rows,
    block_inverse,
    couplings,
    neighbours,
):
    count_x, count_y = lax.axis_size("gx"), lax.axis_size("gy")
    devices = count_x * count_y
    size_x, size_y, depth = source_term.shape
    tiles = size_x * size_y * (depth // TZ)
    blocks, order = block_inverse.shape[:2]
    send, recv = send_tiles[0], recv_rows[0]
    pad = 128 - send.shape[1]
    assert order == 128 and pad >= 0
    if pad:
        send = jnp.pad(send, ((0, 0), (0, pad)), constant_values=tiles)
        recv = jnp.pad(recv, ((0, 0), (0, pad)), constant_values=blocks * order)
    table_rows = tiles // 128
    field = (size_x, size_y, depth)
    hbm = pl.BlockSpec(memory_space=pltpu.HBM)
    vmem = pl.BlockSpec(memory_space=pltpu.VMEM)
    dma = pltpu.SemaphoreType.DMA
    return pl.pallas_call(
        functools.partial(kernel, (count_x, count_y)),
        out_shape=(
            jax.ShapeDtypeStruct(field, F32),
            jax.ShapeDtypeStruct(field, F32),
        ),
        in_specs=[hbm] * 7 + [vmem] * 3,
        out_specs=(vmem, vmem),
        scratch_shapes=[
            pltpu.VMEM(field, F32),
            pltpu.VMEM(field, F32),
            pltpu.VMEM(field, F32),
            pltpu.VMEM(field, F32),
            pltpu.VMEM(field, F32),
            pltpu.VMEM((blocks, order, order), F32),
            pltpu.VMEM(couplings.shape, F32),
            pltpu.VMEM(field, F32),
            pltpu.VMEM(field, F32),
            pltpu.VMEM(field, F32),
            pltpu.VMEM(field, F32),
            pltpu.VMEM(field, F32),
            pltpu.VMEM(field, F32),
            pltpu.VMEM((blocks, order, 2 * order), BF16),
            pltpu.VMEM((blocks, order * couplings.shape[1], 2 * order), BF16),
            pltpu.VMEM((devices // GROUP, 128, GROUP * 128), BF16),
            pltpu.VMEM((devices // GROUP, 128, GROUP * 128), BF16),
            pltpu.VMEM((devices, 128), jnp.int32),
            pltpu.VMEM((table_rows, 128), F32),
            pltpu.VMEM((table_rows, 128), F32),
            pltpu.VMEM((size_y, depth), F32),
            pltpu.VMEM((size_x, 1, depth), F32),
            pltpu.VMEM((size_x, 1, depth), F32),
            pltpu.VMEM((2, 2, size_x, 1, depth), F32),
            pltpu.VMEM((2, 2, size_y, depth), F32),
            pltpu.VMEM((2, 2, size_x, 1, depth), F32),
            pltpu.VMEM((4, devices, 1, 128), F32),
            pltpu.VMEM((4, devices, 1, 128), F32),
            pltpu.VMEM((3, devices, SLOT, 128), F32),
            pltpu.VMEM((3, devices, SLOT, 128), F32),
            pltpu.VMEM((2, 1, 1, 128), F32),
            pltpu.VMEM((2, devices, 1, 128), F32),
            dma((7,)),
            dma((2, 4)),
            dma((2, 4)),
            dma((2,)),
            dma((2,)),
            dma((4,)),
            dma((4,)),
            dma((3,)),
            dma((3,)),
            dma((2,)),
            dma((2,)),
        ],
        compiler_params=pltpu.CompilerParams(
            collective_id=0, has_side_effects=True, vmem_limit_bytes=63500000
        ),
    )(
        source_term,
        mobility_x,
        mobility_y,
        mobility_z,
        bubble_fraction,
        block_inverse,
        couplings,
        send,
        recv,
        neighbours.T,
    )


def solution(mesh):
    return jax.shard_map(
        body,
        mesh=mesh,
        in_specs=(
            P("gx", "gy", None),
            P("gx", "gy", None),
            P("gx", "gy", None),
            P("gx", "gy", None),
            P("gx", "gy", None),
            P("gx", "gy", None),
            P(("gx", "gy"), None, None),
            P(("gx", "gy"), None, None),
            P(("gx", "gy"), None, None),
            P(("gx", "gy"), None, None, None),
            P(("gx", "gy"), None),
        ),
        out_specs=(P("gx", "gy", None), P("gx", "gy", None)),
        check_vma=False,
    )
```

```python
import functools

import jax
import jax.numpy as jnp
from jax import lax
from jax.experimental import pallas as pl
from jax.experimental.pallas import tpu as pltpu
from jax.sharding import PartitionSpec as P

TZ = 128
LINK = 4
SLOT = 4
F32 = jnp.float32
BF16 = jnp.bfloat16
MESH = pl.DeviceIdType.MESH
NT = (((1,), (1,)), ((), ()))
NN = (((1,), (0,)), ((), ()))
GROUP = 8


def log2(value):
    assert value & (value - 1) == 0
    return value.bit_length() - 1


def iota(shape, axis):
    return lax.broadcasted_iota(jnp.int32, shape, axis)


def split_two(value):
    first = value.astype(BF16).astype(F32)
    return first, (value - first).astype(BF16).astype(F32)


def stack_two(value, axis=0):
    return jnp.concatenate(split_two(value), axis=axis).astype(BF16)


def fold_two(value):
    half = value.shape[0] // 2
    return value[:half] + value[half:]


def fold_tiles(value):
    tiles = [
        value[y : y + 8, z : z + 128]
        for y in range(0, value.shape[0], 8)
        for z in range(0, value.shape[1], 128)
    ]
    while len(tiles) > 1:
        tiles = [a + b for a, b in zip(tiles[::2], tiles[1::2])]
    return tiles[0]


def write_one_hots(index_ref, hot_ref):
    def step(block, carry):
        for sub in range(GROUP):
            index = index_ref[pl.ds(block * GROUP + sub, 1), :]
            hot = jnp.where(iota((128, 128), 0) == (index & 127), 1.0, 0.0)
            hot_ref[block, :, sub * 128 : (sub + 1) * 128] = hot.astype(BF16)
        return carry

    lax.fori_loop(0, hot_ref.shape[0], step, 0)


def gather_rows(table, index_ref, hot_ref, out_ref):
    parts = stack_two(table)
    high_count = table.shape[0]

    def step(block, carry):
        picked = fold_two(
            lax.dot_general(parts, hot_ref[block], NN, preferred_element_type=F32)
        )
        for sub in range(GROUP):
            row = block * GROUP + sub
            hit = iota((high_count, 128), 0) == (index_ref[pl.ds(row, 1), :] >> 7)
            mine = picked[:, sub * 128 : (sub + 1) * 128]
            out_ref[row] = jnp.sum(jnp.where(hit, mine, 0.0), axis=0, keepdims=True)
        return carry

    lax.fori_loop(0, hot_ref.shape[0], step, 0)


def scatter_rows(value_ref, index_ref, hot_ref, high_count):
    def step(block, total):
        pieces = []
        for sub in range(GROUP):
            row = block * GROUP + sub
            hit = iota((high_count, 128), 0) == (index_ref[pl.ds(row, 1), :] >> 7)
            pieces.append(stack_two(jnp.where(hit, value_ref[row], 0.0)))
        return total + lax.dot_general(
            jnp.concatenate(pieces, axis=1), hot_ref[block], NT, preferred_element_type=F32
        )

    start = jnp.zeros((2 * high_count, 128), F32)
    return fold_two(lax.fori_loop(0, hot_ref.shape[0], step, start))


def block_vectors(vectors):
    first, second = split_two(vectors)
    out = []
    for q in range(vectors.shape[0]):
        mine = iota(vectors.shape, 0) == q
        top = jnp.where(mine, first, 0.0)
        low = jnp.where(mine, second, 0.0)
        upper = jnp.concatenate([top, top], axis=1)
        lower = jnp.concatenate([low, jnp.zeros_like(low)], axis=1)
        out.append(jnp.concatenate([upper, lower], axis=0).astype(BF16))
    return out


def block_products(vectors, split_ref):
    total = None
    for q, part in enumerate(block_vectors(vectors)):
        term = lax.dot_general(part, split_ref[q], NT, preferred_element_type=F32)
        total = term if total is None else total + term
    return fold_two(total)


def kernel(
    counts,
    source_hbm,
    mob_x_hbm,
    mob_y_hbm,
    mob_z_hbm,
    fraction_hbm,
    inverse_hbm,
    couplings_hbm,
    send_ref,
    recv_ref,
    near_ref,
    out_x,
    out_r,
    res,
    mob_x,
    mob_y,
    mob_z,
    fraction,
    inverse,
    couplings,
    inv_diag,
    zed,
    direction,
    image,
    image_two,
    low_y,
    inverse_split,
    couplings_split,
    send_hot,
    recv_hot,
    send_map,
    tile_table,
    back_table,
    low_mx,
    low_my,
    edge_my,
    edges,
    halo_x,
    halo_y,
    row_send,
    row_recv,
    link_send,
    link_recv,
    sum_send,
    sum_recv,
    load_sem,
    side_send_sem,
    side_recv_sem,
    mob_send_sem,
    mob_recv_sem,
    row_send_sem,
    row_recv_sem,
    link_send_sem,
    link_recv_sem,
    sum_send_sem,
    sum_recv_sem,
):
    count_x, count_y = counts
    devices = count_x * count_y
    at_x, at_y = lax.axis_index("gx"), lax.axis_index("gy")
    me = at_x * count_y + at_y
    size_x, size_y, depth = res.shape
    tiles_z = depth // TZ
    group = 128 // (size_y * tiles_z)
    table_rows = size_x // group
    blocks = inverse.shape[0]
    push_count = near_ref.size

    loads = [
        pltpu.make_async_copy(src, dst, load_sem.at[n])
        for n, (src, dst) in enumerate(
            (
                (source_hbm, res),
                (fraction_hbm, fraction),
                (mob_y_hbm, mob_y),
                (mob_x_hbm, mob_x),
                (mob_z_hbm, mob_z),
                (inverse_hbm, inverse),
                (couplings_hbm, couplings),
            )
        )
    ]
    for load in loads:
        load.start()

    barrier = pltpu.get_barrier_semaphore()

    def peer(step):
        other = lax.rem(me + step, devices)
        return (other // count_y, lax.rem(other, count_y)), other

    def greet(step, carry):
        pl.semaphore_signal(barrier, inc=1, device_id=peer(step)[0], device_id_type=MESH)
        return carry

    low_mx[...] = jnp.zeros_like(low_mx)
    low_my[...] = jnp.zeros_like(low_my)
    halo_x[...] = jnp.zeros_like(halo_x)
    halo_y[...] = jnp.zeros_like(halo_y)
    lax.fori_loop(1, devices, greet, 0)

    def exchange(send, recv, send_sem, recv_sem, same=False):
        def one(step, carry):
            device, other = peer(step)
            pltpu.make_async_remote_copy(
                src_ref=send.at[0 if same else other],
                dst_ref=recv.at[me],
                send_sem=send_sem,
                recv_sem=recv_sem,
                device_id=device,
                device_id_type=MESH,
            ).start()
            return carry

        lax.fori_loop(1, devices, one, 0)
        recv[me] = send[0 if same else me]

    def arrived(recv, recv_sem):
        part = recv.at[pl.ds(0, devices - 1)]
        pltpu.make_async_copy(part, part, recv_sem).wait()

    tile = send_ref[...]
    low = tile & 127
    tile_k = low & (tiles_z - 1)
    tile_j = (low >> log2(tiles_z)) & (size_y - 1)
    tile_g = low >> log2(tiles_z * size_y)
    send_map[...] = (
        (tile - low) + tile_k * (group * size_y) + tile_g * size_y + tile_j
    )

    def stack_tiles(planes):
        return jnp.concatenate(
            [plane[:, k * TZ : (k + 1) * TZ] for k in range(tiles_z) for plane in planes],
            axis=0,
        )

    def coarse_send(phase, field):
        def step(row, carry):
            planes = [fraction[x] * field[x] for x in [row * group + g for g in range(group)]]
            stacked = stack_tiles(planes)
            tile_table[pl.ds(row, 1), :] = jnp.sum(stacked.T, axis=0, keepdims=True)
            return carry

        lax.fori_loop(0, table_rows, step, 0)
        gather_rows(tile_table[...], send_map, send_hot, row_send.at[2 * phase])

    def row_exchange(n):
        exchange(row_send.at[n], row_recv.at[n], row_send_sem.at[n], row_recv_sem.at[n])

    write_one_hots(send_map, send_hot)
    loads[0].wait()
    loads[1].wait()
    coarse_send(0, res)
    pl.semaphore_wait(barrier, devices - 1)
    row_exchange(0)

    near_row = jnp.concatenate([near_ref[k : k + 1] for k in range(near_ref.shape[0])], axis=1)
    target_row = near_row >> log2(blocks)
    down, across = iota((push_count, push_count), 0), iota((push_count, push_count), 1)
    target_col = jnp.sum(
        jnp.where(down == across, target_row.astype(F32), 0.0), axis=1, keepdims=True
    ).astype(jnp.int32)
    earlier = down < across
    same = jnp.where((target_row == target_col) & earlier, 1, 0)
    rank = jnp.sum(same, axis=0, keepdims=True)
    slot = target_row * SLOT + rank
    chosen = iota((devices * SLOT, push_count), 0) == slot
    local = (near_row & (blocks - 1)).astype(F32)
    identity = jnp.sum(jnp.where(chosen, local, 0.0), axis=1, keepdims=True)
    link_send[0] = jnp.broadcast_to(identity, (devices * SLOT, 128)).reshape(
        devices, SLOT, 128
    )
    spread = jnp.where(chosen, 1.0, 0.0).astype(BF16)

    def link_exchange(n):
        exchange(link_send.at[n], link_recv.at[n], link_send_sem.at[n], link_recv_sem.at[n])

    link_exchange(0)

    def side_copy(src, dst, send_sem, recv_sem, shift_x, shift_y):
        return pltpu.make_async_remote_copy(
            src_ref=src,
            dst_ref=dst,
            send_sem=send_sem,
            recv_sem=recv_sem,
            device_id=(at_x + shift_x, at_y + shift_y),
            device_id_type=MESH,
        )

    loads[2].wait()
    loads[3].wait()

    def take_edge(x, carry):
        edge_my[x] = mob_y[x, size_y - 1 : size_y, :]
        return carry

    lax.fori_loop(0, size_x, take_edge, 0)
    copy_mx = side_copy(
        mob_x.at[size_x - 1], low_mx, mob_send_sem.at[0], mob_recv_sem.at[0], 1, 0
    )
    copy_my = side_copy(edge_my, low_my, mob_send_sem.at[1], mob_recv_sem.at[1], 0, 1)
    has_low_x, has_high_x = at_x > 0, at_x < count_x - 1
    has_low_y, has_high_y = at_y > 0, at_y < count_y - 1
    pl.when(has_high_x)(copy_mx.start)
    pl.when(has_high_y)(copy_my.start)

    lane = iota((size_y, depth), 1)
    row_of = iota((size_y, depth), 0)

    def below_z(plane):
        return jnp.where(lane == 0, 0.0, pltpu.roll(plane, 1, 1))

    def above_z(plane):
        return jnp.where(lane == depth - 1, 0.0, pltpu.roll(plane, depth - 1, 1))

    def below_y(plane, edge):
        return jnp.where(row_of == 0, edge, pltpu.roll(plane, 1, 0))

    def above_y(plane, edge):
        return jnp.where(row_of == size_y - 1, edge, pltpu.roll(plane, size_y - 1, 0))

    write_one_hots(recv_ref, recv_hot)
    loads[5].wait()

    def split_inverse(q, carry):
        inverse_split[q] = stack_two(inverse[q], axis=1)
        return carry

    lax.fori_loop(0, blocks, split_inverse, 0)
    loads[6].wait()

    def split_couplings(q, carry):
        couplings_split[q] = stack_two(
            jnp.concatenate([couplings[q, k] for k in range(couplings.shape[1])], axis=0),
            axis=1,
        )
        return carry

    lax.fori_loop(0, blocks, split_couplings, 0)

    def make_diagonal(x, lower):
        here = mob_x[x]
        mob_b, mob_c = mob_y[x], mob_z[x]
        lower_b = below_y(mob_b, low_my[x])
        low_y[x] = lower_b
        value = (here + lower) + (mob_b + lower_b) + (mob_c + below_z(mob_c))
        inv_diag[x] = 1.0 / value
        return here

    def halo_copies(phase):
        out = []
        for side, (there, send, recv_here, shift_x, shift_y, came) in enumerate(
            (
                (has_low_x, 0, 1, -1, 0, has_high_x),
                (has_high_x, 1, 0, 1, 0, has_low_x),
                (has_low_y, 2, 1, 0, -1, has_high_y),
                (has_high_y, 3, 0, 0, 1, has_low_y),
            )
        ):
            field = zed if phase else direction
            if side < 2:
                src = field.at[0 if side == 0 else size_x - 1]
                dst = halo_x.at[phase, recv_here]
            else:
                src = edges.at[phase, side - 2]
                dst = halo_y.at[phase, recv_here]
            copy = side_copy(
                src,
                dst,
                side_send_sem.at[phase, side],
                side_recv_sem.at[phase, side],
                shift_x,
                shift_y,
            )
            out.append((there, came, copy))
        return out

    zero_tile = jnp.zeros((8, 128), F32)

    def coarse_totals(phase):
        n = 2 * phase
        arrived(row_recv.at[n], row_recv_sem.at[n])
        return scatter_rows(row_recv.at[n], recv_ref, recv_hot, blocks)

    def precondition(phase, totals):
        second = 2 * phase + 1
        field = zed if phase else direction
        sweep_one = block_products(totals, inverse_split)
        both = block_products(sweep_one, couplings_split)
        pushed = jnp.concatenate(
            [both[:, k * 128 : (k + 1) * 128] for k in range(couplings.shape[1])], axis=0
        )
        upper, lower = split_two(pushed)
        out_values = lax.dot_general(
            spread, upper.astype(BF16), NN, preferred_element_type=F32
        ) + lax.dot_general(spread, lower.astype(BF16), NN, preferred_element_type=F32)
        link_send[1 + phase] = out_values.reshape(devices, SLOT, 128)
        link_exchange(1 + phase)
        if phase == 0:
            loads[4].wait()
            pl.when(has_low_x)(copy_mx.wait_recv)
            pl.when(has_low_y)(copy_my.wait_recv)
            lax.fori_loop(0, size_x, make_diagonal, low_mx[...])
            arrived(link_recv.at[0], link_recv_sem.at[0])
        names = link_recv[0].reshape(devices * SLOT, 128).T[:blocks]
        gather_in = jnp.where(
            names == iota((blocks, devices * SLOT), 0).astype(F32), 1.0, 0.0
        ).astype(BF16)
        arrived(link_recv.at[1 + phase], link_recv_sem.at[1 + phase])
        values = stack_two(link_recv[1 + phase].reshape(devices * SLOT, 128), axis=1)
        summed = lax.dot_general(gather_in, values, NN, preferred_element_type=F32)
        coupled = summed[:, :128] + summed[:, 128:]
        sweep_two = block_products(totals - coupled, inverse_split)
        gather_rows(sweep_two, recv_ref, recv_hot, row_send.at[second])
        row_exchange(second)
        arrived(row_recv.at[second], row_recv_sem.at[second])
        back_table[...] = scatter_rows(
            row_recv.at[second], send_map, send_hot, table_rows
        )

        def step(row, total):
            stacked = jnp.broadcast_to(back_table[pl.ds(row, 1), :], (128, 128)).T
            for g in range(group):
                x = row * group + g
                tiles = [
                    stacked[(k * group + g) * size_y : (k * group + g + 1) * size_y]
                    for k in range(tiles_z)
                ]
                here = res[x]
                value = fraction[x] * jnp.concatenate(tiles, axis=1) + here * inv_diag[x]
                field[x] = value
                edges[phase, 0, x] = value[0:1]
                edges[phase, 1, x] = value[size_y - 1 : size_y]
                total = total + fold_tiles(here * value)
            return total

        return jnp.sum(lax.fori_loop(0, table_rows, step, zero_tile))

    def apply_operator(phase, copies):
        field = zed if phase else direction
        result = image_two if phase else image
        for there, came, copy in copies:
            pl.when(there)(copy.start)
        def plane_step(x, below, here, above, lower):
            mob_a, mob_b, mob_c = mob_x[x], mob_y[x], mob_z[x]
            part_x = mob_a * (above - here) - lower * (here - below)
            part_y = mob_b * (above_y(here, 0.0) - here) - low_y[x] * (
                here - below_y(here, 0.0)
            )
            flux = mob_c * (above_z(here) - here)
            value = -(part_x + part_y + (flux - below_z(flux)))
            result[x] = value
            one = fold_tiles(here * value)
            return one, fold_tiles(here * image[x]) if phase else one, mob_a

        def step(x, carry):
            below, here, lower, total, cross = carry
            above = field[x + 1]
            one, two, lower = plane_step(x, below, here, above, lower)
            return here, above, lower, total + one, cross + two

        zero_plane = jnp.zeros((size_y, depth), F32)
        below, here, lower, total, cross = lax.fori_loop(
            0,
            size_x - 1,
            step,
            (zero_plane, field[0], low_mx[...], zero_tile, zero_tile),
        )
        one, two, lower = plane_step(size_x - 1, below, here, zero_plane, lower)
        total, cross = total + one, cross + two

        for there, came, copy in copies:
            pl.when(came)(copy.wait_recv)
        for x, weight, beside in (
            (0, low_mx[...], halo_x[phase, 0]),
            (size_x - 1, mob_x[size_x - 1], halo_x[phase, 1]),
        ):
            change = weight * beside
            result[x] = result[x] - change
            total = total - fold_tiles(field[x] * change)

        def edge_step(block, total):
            for sub in range(4):
                x = block * 4 + sub
                for y, weight, beside in (
                    (0, low_y, halo_y[phase, 0, x]),
                    (size_y - 1, mob_y, halo_y[phase, 1, x]),
                ):
                    change = weight[x, y : y + 1, :] * beside
                    result[x, y : y + 1, :] = result[x, y : y + 1, :] - change
                    total = total - field[x, y : y + 1, :] * change
            return total

        edge_total = lax.fori_loop(0, size_x // 4, edge_step, jnp.zeros((1, depth), F32))
        return jnp.sum(total) + jnp.sum(edge_total), jnp.sum(cross)

    place = iota((1, 128), 1)

    def start_sums(phase, values):
        row = jnp.zeros((1, 128), F32)
        for n, value in enumerate(values):
            row = jnp.where(place == n, value, row)
        sum_send[phase, 0] = row
        exchange(
            sum_send.at[phase],
            sum_recv.at[phase],
            sum_send_sem.at[phase],
            sum_recv_sem.at[phase],
            same=True,
        )

    def end_sums(phase, count):
        arrived(sum_recv.at[phase], sum_recv_sem.at[phase])
        totals = [sum_recv[phase, n] for n in range(4)]
        for n in range(4, devices):
            totals[n % 4] = totals[n % 4] + sum_recv[phase, n]
        total = (totals[0] + totals[1]) + (totals[2] + totals[3])
        return [
            jnp.sum(jnp.where(place == n, total, 0.0), axis=1, keepdims=True)
            for n in range(count)
        ]

    copies_0, copies_1 = halo_copies(0), halo_copies(1)
    totals = coarse_totals(0)
    rz_part = precondition(0, totals)
    energy_part, _ = apply_operator(0, copies_0)
    start_sums(0, (rz_part, energy_part))

    coarse_send(1, image)
    row_exchange(2)
    rz, energy = end_sums(0, 2)
    alpha = rz / energy

    def update_residual(x, carry):
        res[x] = res[x] - alpha * image[x]
        return carry

    lax.fori_loop(0, size_x, update_residual, 0)
    totals = totals - alpha * coarse_totals(1)
    next_part = precondition(1, totals)
    own_part, cross_part = apply_operator(1, copies_1)
    start_sums(1, (next_part, own_part, cross_part))
    rz_next, own, cross = end_sums(1, 3)
    beta = rz_next / rz
    alpha_two = rz_next / (own + beta * (2.0 * cross + beta * energy))

    def finish(x, carry):
        first = direction[x]
        out_x[x] = alpha * first + alpha_two * (zed[x] + beta * first)
        out_r[x] = res[x] - alpha_two * (image_two[x] + beta * image[x])
        return carry

    lax.fori_loop(0, size_x, finish, 0)
    pl.when(has_high_x)(copy_mx.wait_send)
    pl.when(has_high_y)(copy_my.wait_send)
    for there, came, copy in copies_0 + copies_1:
        pl.when(there)(copy.wait_send)
    for n in range(4):
        arrived(row_send.at[n], row_send_sem.at[n])
    for n in range(3):
        arrived(link_send.at[n], link_send_sem.at[n])
    for n in range(2):
        arrived(sum_recv.at[n], sum_send_sem.at[n])


def hand_on(x_ref, r_ref, out_x, out_r):
    out_x[...] = x_ref[...]
    out_r[...] = r_ref[...]


def body(
    source_term,
    mobility_x,
    mobility_y,
    mobility_z,
    bubble_fraction,
    tile_labels,
    send_tiles,
    recv_rows,
    block_inverse,
    couplings,
    neighbours,
):
    count_x, count_y = lax.axis_size("gx"), lax.axis_size("gy")
    devices = count_x * count_y
    size_x, size_y, depth = source_term.shape
    tiles = size_x * size_y * (depth // TZ)
    blocks, order = block_inverse.shape[:2]
    send, recv = send_tiles[0], recv_rows[0]
    pad = 128 - send.shape[1]
    assert order == 128 and pad >= 0
    if pad:
        send = jnp.pad(send, ((0, 0), (0, pad)), constant_values=tiles)
        recv = jnp.pad(recv, ((0, 0), (0, pad)), constant_values=blocks * order)
    table_rows = tiles // 128
    field = (size_x, size_y, depth)
    hbm = pl.BlockSpec(memory_space=pltpu.HBM)
    vmem = pl.BlockSpec(memory_space=pltpu.VMEM)
    dma = pltpu.SemaphoreType.DMA
    results = pl.pallas_call(
        functools.partial(kernel, (count_x, count_y)),
        out_shape=(
            jax.ShapeDtypeStruct(field, F32),
            jax.ShapeDtypeStruct(field, F32),
        ),
        in_specs=[hbm] * 7 + [vmem] * 3,
        out_specs=(vmem, vmem),
        scratch_shapes=[
            pltpu.VMEM(field, F32),
            pltpu.VMEM(field, F32),
            pltpu.VMEM(field, F32),
            pltpu.VMEM(field, F32),
            pltpu.VMEM(field, F32),
            pltpu.VMEM((blocks, order, order), F32),
            pltpu.VMEM(couplings.shape, F32),
            pltpu.VMEM(field, F32),
            pltpu.VMEM(field, F32),
            pltpu.VMEM(field, F32),
            pltpu.VMEM(field, F32),
            pltpu.VMEM(field, F32),
            pltpu.VMEM(field, F32),
            pltpu.VMEM((blocks, order, 2 * order), BF16),
            pltpu.VMEM((blocks, order * couplings.shape[1], 2 * order), BF16),
            pltpu.VMEM((devices // GROUP, 128, GROUP * 128), BF16),
            pltpu.VMEM((devices // GROUP, 128, GROUP * 128), BF16),
            pltpu.VMEM((devices, 128), jnp.int32),
            pltpu.VMEM((table_rows, 128), F32),
            pltpu.VMEM((table_rows, 128), F32),
            pltpu.VMEM((size_y, depth), F32),
            pltpu.VMEM((size_x, 1, depth), F32),
            pltpu.VMEM((size_x, 1, depth), F32),
            pltpu.VMEM((2, 2, size_x, 1, depth), F32),
            pltpu.VMEM((2, 2, size_y, depth), F32),
            pltpu.VMEM((2, 2, size_x, 1, depth), F32),
            pltpu.VMEM((4, devices, 1, 128), F32),
            pltpu.VMEM((4, devices, 1, 128), F32),
            pltpu.VMEM((3, devices, SLOT, 128), F32),
            pltpu.VMEM((3, devices, SLOT, 128), F32),
            pltpu.VMEM((2, 1, 1, 128), F32),
            pltpu.VMEM((2, devices, 1, 128), F32),
            dma((7,)),
            dma((2, 4)),
            dma((2, 4)),
            dma((2,)),
            dma((2,)),
            dma((4,)),
            dma((4,)),
            dma((3,)),
            dma((3,)),
            dma((2,)),
            dma((2,)),
        ],
        compiler_params=pltpu.CompilerParams(
            collective_id=0, has_side_effects=True, vmem_limit_bytes=63500000
        ),
    )(
        source_term,
        mobility_x,
        mobility_y,
        mobility_z,
        bubble_fraction,
        block_inverse,
        couplings,
        send,
        recv,
        neighbours.T,
    )
    part = pl.BlockSpec((size_x // 4, size_y, depth), lambda n: (n, 0, 0))
    return pl.pallas_call(
        hand_on,
        grid=(4,),
        out_shape=(jax.ShapeDtypeStruct(field, F32),) * 2,
        in_specs=[part] * 2,
        out_specs=(part, part),
    )(*results)


def solution(mesh):
    return jax.shard_map(
        body,
        mesh=mesh,
        in_specs=(
            P("gx", "gy", None),
            P("gx", "gy", None),
            P("gx", "gy", None),
            P("gx", "gy", None),
            P("gx", "gy", None),
            P("gx", "gy", None),
            P(("gx", "gy"), None, None),
            P(("gx", "gy"), None, None),
            P(("gx", "gy"), None, None),
            P(("gx", "gy"), None, None, None),
            P(("gx", "gy"), None),
        ),
        out_specs=(P("gx", "gy", None), P("gx", "gy", None)),
        check_vma=False,
    )
```
